32 devices in a mesh: sx: 4 (over z), sy: 8 (over y, x, core).
Axes of the slice: x: 2, y: 2, z: 4, core: 2. Of those that a mesh axis runs over, the one named last changes fastest.
Arguments:
- residual: bfloat16 [4, 8, 2048, 128], P('sx', 'sy'), may hold values from -6 to 6
- weights: float32 [4, 8, 2048], P('sx', 'sy'), may hold values from 0.1 to 1.9
- blocks: bfloat16 [4, 8, 16, 4, 128, 128], P('sx', 'sy'), may hold values from -0.25 to 0.25
- pattern: int32 [4, 8, 16, 4], P('sx', 'sy'), may hold values from 0 to 15
- primal_basis: bfloat16 [4, 8, 2048, 64], P('sx', 'sy'), may hold values from -0.25 to 0.25
- coarse_inverse: float32 [4, 512, 512], P('sx', 'sy'), may hold values from -0.25 to 0.25
- coarse_rows: int32 [4, 512], P('sx'), may hold values from 0 to 511, each once within a row
- shared_lists: int32 [4, 8, 4, 512], P('sx', 'sy'), may hold values from 0 to 511, each once within a row
Outputs:
- preconditioned: bfloat16 [4, 8, 2048, 128], P('sx', 'sy')
The draws below stay inside these ranges and needn't reach their ends.
Inputs may be any that keep to these rules, and one draw needn't show every extreme that they name: `pattern`: block column indices; one block row may name a column twice. `coarse_rows`: each row of a grid row's map names every coarse row once. `shared_lists`: each face's list names every row of the face once.
All inputs are finite; a program needn't handle non-finite values.
Results may differ from the reference program's by a relative error of at most 0.0085.
Values may be sent and summed in bfloat16 or wider, within the bound.
A program may use at most 64 MiB of HBM per device.

```python
import jax
import jax.numpy as jnp
from jax import lax

FACE = 512
BLK = 128
KNZ = 4
NPRIM = 64
NVEC = 128
NI = 2048
NB = 16
NCR = 512
N_SX = 4
N_SY = 8


def set_ends(values, key, smallest, largest):
    longest = values.shape.index(max(values.shape))
    spots = []
    for shift in (0, 1):
        where = [jax.random.randint(jax.random.fold_in(key, axis), (), 0, length) for axis, length in enumerate(values.shape)]
        where[longest] = (where[longest] + shift) % values.shape[longest]
        spots.append(tuple(where))
    return values.at[spots[0]].set(smallest).at[spots[1]].set(largest)


def levels(own_key, shape, cuts, smallest, top_value):
    loudness, own = 1.0, jax.random.fold_in(own_key, 6)
    for dim, parts in cuts:
        steps = jnp.exp(jax.random.uniform(jax.random.fold_in(own, dim), (parts,), jnp.float32, smallest / len(cuts), top_value / len(cuts)))
        loudness = loudness * jnp.repeat(steps, shape[dim] // parts).reshape([-1 if axis == dim else 1 for axis in range(len(shape))])
    return loudness


def centred(own_key, shape, deviation, most, cuts=(), kind=jnp.bfloat16):
    values = deviation * jax.random.normal(own_key, shape, jnp.float32)
    if cuts:
        values = values * levels(own_key, shape, cuts, -0.22, 0.18)
    return jnp.clip(values, -most, most).astype(kind)


def setup_inputs(seed: int = 0) -> dict:
    key_of = jax.random.split(jax.random.key(seed), 9)
    return {
        "residual": centred(key_of[0], (N_SX, N_SY, NI, NVEC), 1.0, 6.0, ((0, 4), (1, 8))),
        "weights": jnp.clip(1.0 + 0.18 * jax.random.normal(key_of[1], (N_SX, N_SY, NI), jnp.float32), 0.1, 1.9),
        "blocks": centred(key_of[2], (N_SX, N_SY, NB, KNZ, BLK, BLK), (BLK * KNZ) ** -0.5, 0.25, ((0, 4), (1, 8))),
        "pattern": set_ends(jax.random.randint(key_of[3], (N_SX, N_SY, NB, KNZ), 0, NB), jax.random.fold_in(key_of[3], 1), 0, NB - 1).astype(jnp.int32),
        "primal_basis": centred(key_of[4], (N_SX, N_SY, NI, NPRIM), (NI // 4) ** -0.5, 0.25, ((0, 4), (1, 8))),
        "coarse_inverse": centred(key_of[5], (N_SX, NCR, NCR), NCR ** -0.5, 0.25, ((0, 4), (1, 8)), jnp.float32),
        "coarse_rows": jax.vmap(lambda own: jax.random.permutation(own, NCR))(jax.random.split(key_of[6], N_SX)).reshape((N_SX, NCR)).astype(jnp.int32),
        "shared_lists": jax.vmap(lambda own: jax.random.permutation(own, FACE))(jax.random.split(key_of[7], N_SX * N_SY * 4)).reshape((N_SX, N_SY, 4, FACE)).astype(jnp.int32),
    }


def subdomain_part(items):
    residual, weights, blocks, pattern, primal_basis = items
    weighted = (weights[:, None] * residual.astype(jnp.float32)).astype(jnp.bfloat16)
    pieces = weighted.reshape(NB, BLK, NVEC)[pattern]
    solved = jnp.einsum('bkrc,bkcn->brn', blocks.astype(jnp.float32), pieces.astype(jnp.float32)).reshape(NI, NVEC)
    primal_vals = jnp.dot(primal_basis.T, weighted, preferred_element_type=jnp.float32)
    return solved, primal_vals


def place_rows(order, values):
    return jnp.zeros_like(values).at[order].set(values)


def pick_rows(values, order):
    return values[order]


def correct_part(items):
    solved, weights, primal_basis, primal_sol = items
    correction = jnp.dot(primal_basis, primal_sol, preferred_element_type=jnp.float32)
    return weights[:, None] * (solved + correction)


def reference(residual, weights, blocks, pattern, primal_basis, coarse_inverse, coarse_rows, shared_lists):
    count = N_SX * N_SY
    flat_w = weights.reshape(count, NI)
    flat_basis = primal_basis.reshape(count, NI, NPRIM)
    solved, primal_vals = lax.map(subdomain_part, (residual.reshape(count, NI, NVEC), flat_w, blocks.reshape(count, NB, KNZ, BLK, BLK), pattern.reshape(count, NB, KNZ), flat_basis))
    primal_vals = primal_vals.reshape(N_SX, NCR, NVEC)
    coarse_rhs = jax.vmap(place_rows)(coarse_rows, primal_vals)
    coarse_sol = jnp.einsum('imn,inv->imv', coarse_inverse, coarse_rhs, precision=lax.Precision.HIGHEST)
    primal_sol = jax.vmap(pick_rows)(coarse_sol, coarse_rows).astype(jnp.bfloat16).reshape(count, NPRIM, NVEC)
    value = lax.map(correct_part, (solved, flat_w, flat_basis, primal_sol))
    value = value.reshape(N_SX, N_SY, 4, FACE, NVEC)
    from_north = jnp.pad(value[:-1, :, 1], ((1, 0), (0, 0), (0, 0), (0, 0)))
    from_south = jnp.pad(value[1:, :, 0], ((0, 1), (0, 0), (0, 0), (0, 0)))
    from_west = jnp.pad(value[:, :-1, 3], ((0, 0), (1, 0), (0, 0), (0, 0)))
    from_east = jnp.pad(value[:, 1:, 2], ((0, 0), (0, 1), (0, 0), (0, 0)))
    picker = jax.vmap(jax.vmap(pick_rows))
    across = jnp.stack([picker(from_north, shared_lists[:, :, 0]), picker(from_south, shared_lists[:, :, 1]), picker(from_west, shared_lists[:, :, 2]), picker(from_east, shared_lists[:, :, 3])], axis=2)
    total = value + across
    return total.reshape(N_SX, N_SY, NI, NVEC).astype(jnp.bfloat16)
```

```python
import functools

import jax
import jax.numpy as jnp
from jax import lax
from jax.experimental import pallas as pl
from jax.experimental.pallas import tpu as pltpu
from jax.sharding import PartitionSpec as P

MESH = pl.DeviceIdType.MESH
F32 = jnp.float32
BF16 = jnp.bfloat16
LANES = 128
OPPOSITE = (1, 0, 3, 2)


def down_rows(row):
    return jnp.broadcast_to(row, (LANES, LANES)).T


def kernel(
    n_sx, n_sy,
    res_hbm, w_hbm, blocks_hbm, pat_hbm, basis_hbm, inv_hbm, ord_hbm, sh_hbm,
    out,
    res, w_ref, basis, blocks, inv, ord_ref, sh_ref, pat_ref,
    wcol, weighted, acc, comb, onehot, inv_perm, pick,
    gath, csol, psol, face_out, basis_out, face_in, basis_in, psol_in,
    in_sem, blk_sem, iv_s, iv_r, pv_s, pv_r, cs_s, cs_r, fb_s, fb_r, fw_s, fw_r,
    sp_s, sp_r, ps_s, ps_r,
):
    i, j = lax.axis_index("sx"), lax.axis_index("sy")
    nb, knz, blk, _ = blocks.shape
    nprim = basis.shape[0]
    ncr = gath.shape[0]
    ni, nvec = res.shape
    face = ni // 4
    per = face // blk
    n_hub = n_sy // 2
    pair = 2 * nprim

    c, side = j // 2, lax.rem(j, 2)
    is_hub, is_leaf = side == 1, side == 0
    sibling = (i, j + 1 - 2 * side)

    loads = [
        pltpu.make_async_copy(source, target, in_sem.at[n])
        for n, (source, target) in enumerate(
            (
                (w_hbm, w_ref), (basis_hbm, basis), (res_hbm, res), (ord_hbm, ord_ref),
                (sh_hbm, sh_ref), (pat_hbm, pat_ref),
                (inv_hbm, inv.at[pl.ds(nprim, nprim)]),
            )
        )
    ]
    load_w, load_basis, load_res, load_ord, load_sh, load_pat, load_inv = loads
    load_blocks = [
        pltpu.make_async_copy(
            blocks_hbm.at[pl.ds(f * per, per)], blocks.at[pl.ds(f * per, per)], blk_sem.at[f]
        )
        for f in range(4)
    ]
    for copy in loads[:3]:
        copy.start()

    has = (i > 0, i < n_sx - 1, j > 0, j < n_sy - 1)
    there = ((i - 1, j), (i + 1, j), (i, j - 1), (i, j + 1))

    def hub_of(step):
        return lax.rem(c + step, n_hub)

    barrier = pltpu.get_barrier_semaphore()

    def signal(device):
        pl.semaphore_signal(barrier, inc=1, device_id=device, device_id_type=MESH)

    signal(sibling)

    def greet(step, carry):
        signal((i, 2 * hub_of(step) + 1))
        return carry

    lax.fori_loop(1, n_hub, greet, 0, unroll=n_hub <= 4)
    for f in (0, 1):

        @pl.when(has[f])
        def _():
            signal(there[f])

        @pl.when(jnp.logical_and(has[f], is_leaf))
        def _():
            signal((there[f][0], j + 1))

    @pl.when(is_hub)
    def _():
        def greet_leaf(step, carry):
            signal((i, 2 * hub_of(step)))
            return carry

        lax.fori_loop(1, n_hub, greet_leaf, 0, unroll=n_hub <= 4)

    for copy in loads[3:] + load_blocks:
        copy.start()

    def remote(src, dst, send, recv, device):
        return pltpu.make_async_remote_copy(
            src_ref=src, dst_ref=dst, send_sem=send, recv_sem=recv,
            device_id=device, device_id_type=MESH,
        )

    def basis_copy(f):
        g = OPPOSITE[f]
        return remote(basis_out.at[f], basis_in.at[g], fb_s.at[f], fb_r.at[g], there[f])

    def face_copy(f):
        g = OPPOSITE[f]
        return remote(face_out.at[f], face_in.at[g], fw_s.at[f], fw_r.at[g], there[f])

    def inv_copy():
        return remote(
            inv_hbm, inv.at[pl.ds(0, nprim)], iv_s.at[0], iv_r.at[0], sibling
        )

    def pv_copy(slot, hub):
        rows = pl.ds(pl.multiple_of(slot * nprim, nprim), nprim)
        return remote(
            gath.at[rows], gath.at[rows], pv_s.at[hub], pv_r.at[slot], (i, 2 * hub + 1)
        )

    def csol_copy(slot, hub):
        rows = pl.ds(pl.multiple_of(slot * pair, pair), pair)
        return remote(
            csol.at[rows], csol.at[rows], cs_s.at[hub], cs_r.at[slot], (i, 2 * hub + 1)
        )

    def pair_copy():
        rows = pl.ds(0, 3 * nprim)
        return remote(psol.at[rows], psol.at[rows], sp_s.at[0], sp_r.at[0], sibling)

    def psol_copy(f, half):
        rows = pl.ds((1 + half) * nprim, nprim)
        return remote(
            psol.at[rows], psol_in.at[OPPOSITE[f]], ps_s.at[f, half],
            ps_r.at[OPPOSITE[f]], (there[f][0], 2 * c + half),
        )

    for f in range(4):

        @pl.when(jnp.logical_not(has[f]))
        def _():
            face_in[f] = jnp.zeros(face_in.shape[1:], BF16)
            basis_in[f] = jnp.zeros(basis_in.shape[1:], BF16)
            if f < 2:
                psol_in[f] = jnp.zeros(psol_in.shape[1:], BF16)

    load_w.wait()
    load_basis.wait()
    for f in range(4):
        at = slice(f * face, (f + 1) * face)
        basis_out[f] = (w_ref[0:1, at] * basis[:, at].astype(F32)).astype(BF16)
    load_res.wait()
    pv = jnp.zeros((nprim, nvec), F32)
    for f in range(4):
        pv += jnp.dot(
            basis_out[f], res[f * face : (f + 1) * face, :], preferred_element_type=F32
        )
    own = pl.ds(pl.multiple_of(j * nprim, nprim), nprim)
    gath[own, :] = pv.astype(BF16)

    near = has[0].astype(jnp.int32) + has[1].astype(jnp.int32)
    pl.semaphore_wait(barrier, jnp.where(is_hub, n_sy - 1 + 2 * near, n_hub + near))

    @pl.when(is_leaf)
    def _():
        pv_copy(j, c).start()

    def send_pv(step, carry):
        pv_copy(j, hub_of(step)).start()
        return carry

    lax.fori_loop(1, n_hub, send_pv, 0, unroll=n_hub <= 4)

    @pl.when(is_leaf)
    def _():
        inv_copy().start()

    for f in range(4):

        @pl.when(has[f])
        def _():
            basis_copy(f).start()

    for b in range(nb):
        rows = slice(b * blk, (b + 1) * blk)
        wcol[b] = down_rows(w_ref[0:1, rows])
        weighted[b] = (wcol[b] * res[rows, :].astype(F32)).astype(BF16)

    load_pat.wait()
    for f in range(4):
        load_blocks[f].wait()
        for b in range(f * per, (f + 1) * per):
            left = jnp.concatenate([blocks[b, k] for k in range(knz)], axis=1)
            right = jnp.concatenate([weighted[pat_ref[k, b]] for k in range(knz)], axis=0)
            solved = wcol[b] * jnp.dot(left, right, preferred_element_type=F32)
            rows = slice(b * blk, (b + 1) * blk)
            acc[rows, :] = solved
            face_out[f, (b - f * per) * blk : (b - f * per + 1) * blk, :] = solved.astype(BF16)

        @pl.when(has[f])
        def _():
            face_copy(f).start()

    load_inv.wait()
    load_ord.wait()
    load_sh.wait()

    @pl.when(is_hub)
    def _():
        for m, who in enumerate((jnp.maximum(c - 1, 0), c, jnp.minimum(c + 1, n_hub - 1))):
            at = pl.ds(pl.multiple_of(who * LANES, LANES), LANES)
            col = down_rows(ord_ref[:, at].astype(F32))
            lane = lax.broadcasted_iota(jnp.int32, (LANES, LANES), 1).astype(F32)
            low = nprim if m == 0 else 0
            high = nprim if m == 2 else pair
            base = m * pair - nprim
            for q in range(ncr // LANES):
                hit = jnp.where(col == lane + float(q * LANES), 1.0, 0.0).astype(BF16)
                pick[base + low : base + high, q * LANES : (q + 1) * LANES] = hit[low:high, :]

        chunk = 512 if ncr <= 512 else LANES
        inv_copy().wait_recv()
        inv16 = inv[...].astype(BF16)

        def permute_columns(q, carry):
            at = pl.ds(pl.multiple_of(q * chunk, chunk), chunk)
            hit = lax.broadcasted_iota(jnp.int32, (ncr, chunk), 0) == ord_ref[:, at]
            inv_perm[:, at] = jnp.dot(
                inv16, jnp.where(hit, 1.0, 0.0).astype(BF16), preferred_element_type=F32
            ).astype(BF16)
            return carry

        lax.fori_loop(0, ncr // chunk, permute_columns, 0)

        def wait_pv(step, carry):
            slot = lax.rem(j + step, n_sy)
            pv_copy(slot, c).wait_recv()
            return carry

        lax.fori_loop(1, n_sy, wait_pv, 0, unroll=n_sy <= 8)
        mine = pl.ds(pl.multiple_of(c * pair, pair), pair)
        csol[mine, :] = jnp.dot(
            inv_perm[...], gath[...], preferred_element_type=F32
        ).astype(BF16)

        def send_csol(step, carry):
            csol_copy(c, hub_of(step)).start()
            return carry

        lax.fori_loop(1, n_hub, send_csol, 0, unroll=n_hub <= 4)

    wide_lane = lax.broadcasted_iota(jnp.int32, (LANES, face), 1).astype(F32)
    for f in (2, 3, 0, 1):
        for q in range(face // LANES):
            at = slice(q * LANES, (q + 1) * LANES)
            col = down_rows(sh_ref[f : f + 1, at].astype(F32))
            col = jnp.concatenate([col] * (face // LANES), axis=1)
            onehot[f, at, :] = jnp.where(col == wide_lane, 1.0, 0.0).astype(BF16)

        @pl.when(has[f])
        def _():
            basis_copy(OPPOSITE[f]).wait_recv()

        moved = lax.dot_general(
            basis_in[f], onehot[f], (((1,), (1,)), ((), ())), preferred_element_type=F32
        )
        both = jnp.concatenate([basis_out[f].astype(F32), moved], axis=0)
        comb[f] = both.T.astype(BF16)

    @pl.when(is_hub)
    def _():
        def wait_csol(step, carry):
            hub = hub_of(step)
            csol_copy(hub, hub).wait_recv()
            return carry

        lax.fori_loop(1, n_hub, wait_csol, 0, unroll=n_hub <= 4)
        psol[...] = jnp.dot(pick[...], csol[...], preferred_element_type=F32).astype(BF16)
        for half in (0, 1):
            for f in (0, 1):

                @pl.when(has[f])
                def _():
                    psol_copy(f, half).start()

        pair_copy().start()

    for f in (2, 3, 0, 1):

        @pl.when(has[f])
        def _():
            face_copy(OPPOSITE[f]).wait_recv()

        rows = slice(f * face, (f + 1) * face)
        acc[rows, :] = acc[rows, :] + jnp.dot(
            onehot[f], face_in[f], preferred_element_type=F32
        )

    @pl.when(is_leaf)
    def _():
        pair_copy().wait_recv()

    base = side * nprim

    def psol_rows(m):
        return psol[pl.ds(pl.multiple_of(base + m * nprim, nprim), nprim), :]

    for f in (2, 3, 0, 1):
        if f < 2:

            @pl.when(has[f])
            def _():
                psol_copy(OPPOSITE[f], 0).wait_recv()

        other = psol_in[f] if f < 2 else psol_rows(0 if f == 2 else 2)
        both = jnp.concatenate([psol_rows(1), other], axis=0)
        rows = slice(f * face, (f + 1) * face)
        out[rows, :] = (
            acc[rows, :]
            + jnp.dot(comb[f], both, preferred_element_type=F32)
        ).astype(BF16)

    def drain_pv(step, carry):
        pv_copy(j, hub_of(step)).wait_send()
        return carry

    lax.fori_loop(1, n_hub, drain_pv, 0, unroll=n_hub <= 4)

    @pl.when(is_leaf)
    def _():
        pv_copy(j, c).wait_send()
        inv_copy().wait_send()

    @pl.when(is_hub)
    def _():
        def drain_csol(step, carry):
            csol_copy(c, hub_of(step)).wait_send()
            return carry

        lax.fori_loop(1, n_hub, drain_csol, 0, unroll=n_hub <= 4)
        pair_copy().wait_send()
        for half in (0, 1):
            for f in (0, 1):

                @pl.when(has[f])
                def _():
                    psol_copy(f, half).wait_send()

    for f in range(4):

        @pl.when(has[f])
        def _():
            basis_copy(f).wait_send()
            face_copy(f).wait_send()


def body(
    n_sx, n_sy,
    residual, weights, blocks, pattern, primal_basis, coarse_inverse, coarse_rows, shared_lists,
):
    ni, nvec = residual.shape[2:]
    nb, knz, blk = blocks.shape[2:5]
    nprim = primal_basis.shape[-1]
    ncr = coarse_rows.shape[-1]
    face = shared_lists.shape[-1]
    n_hub = n_sy // 2
    hbm = pl.BlockSpec(memory_space=pltpu.HBM)
    vmem = pl.BlockSpec(memory_space=pltpu.VMEM)
    dma = pltpu.SemaphoreType.DMA
    limit = 64 * 1024 * 1024 - 65536 - ni * nvec * 2
    total = pl.pallas_call(
        functools.partial(kernel, n_sx, n_sy),
        out_shape=pltpu.VMEM((ni, nvec), BF16),
        in_specs=[hbm] * 8,
        out_specs=vmem,
        scratch_shapes=[
            pltpu.VMEM((ni, nvec), BF16),
            pltpu.VMEM((1, ni), F32),
            pltpu.VMEM((nprim, ni), BF16),
            pltpu.VMEM((nb, knz, blk, blk), BF16),
            pltpu.VMEM((2 * nprim, ncr), F32),
            pltpu.VMEM((1, ncr), jnp.int32),
            pltpu.VMEM((4, face), jnp.int32),
            pltpu.SMEM((knz, nb), jnp.int32),
            pltpu.VMEM((nb, blk, LANES), F32),
            pltpu.VMEM((nb, blk, nvec), BF16),
            pltpu.VMEM((ni, nvec), F32),
            pltpu.VMEM((4, face, 2 * nprim), BF16),
            pltpu.VMEM((4, face, face), BF16),
            pltpu.VMEM((2 * nprim, ncr), BF16),
            pltpu.VMEM((4 * nprim, ncr), BF16),
            pltpu.VMEM((ncr, nvec), BF16),
            pltpu.VMEM((ncr, nvec), BF16),
            pltpu.VMEM((4 * nprim, nvec), BF16),
            pltpu.VMEM((4, face, nvec), BF16),
            pltpu.VMEM((4, nprim, face), BF16),
            pltpu.VMEM((4, face, nvec), BF16),
            pltpu.VMEM((4, nprim, face), BF16),
            pltpu.VMEM((2, nprim, nvec), BF16),
            dma((7,)), dma((4,)), dma((1,)), dma((1,)),
            dma((n_hub,)), dma((n_sy,)), dma((n_hub,)), dma((n_hub,)),
            dma((4,)), dma((4,)), dma((4,)), dma((4,)),
            dma((1,)), dma((1,)), dma((2, 2)), dma((2,)),
        ],
        compiler_params=pltpu.CompilerParams(
            collective_id=0, has_side_effects=True, vmem_limit_bytes=limit
        ),
    )(
        residual[0, 0], weights[0], blocks[0, 0], pattern[0, 0].T, primal_basis[0, 0].T,
        coarse_inverse[0], coarse_rows, shared_lists[0, 0],
    )
    pieces = 4

    def hand_over(held, target, sem):
        step = ni // pieces
        writes = [
            pltpu.make_async_copy(
                held.at[pl.ds(p * step, step)], target.at[pl.ds(p * step, step)], sem.at[p]
            )
            for p in range(pieces)
        ]
        for copy in writes:
            copy.start()
        for copy in writes:
            copy.wait()

    total = pl.pallas_call(
        hand_over,
        out_shape=jax.ShapeDtypeStruct((ni, nvec), BF16),
        in_specs=[vmem],
        out_specs=hbm,
        scratch_shapes=[dma((pieces,))],
        compiler_params=pltpu.CompilerParams(vmem_limit_bytes=4 * 1024 * 1024),
    )(total)
    return total[None, None]


def solution(mesh):
    return jax.shard_map(
        functools.partial(body, mesh.shape["sx"], mesh.shape["sy"]),
        mesh=mesh,
        in_specs=(
            P("sx", "sy", None, None),
            P("sx", "sy", None),
            P("sx", "sy", None, None, None, None),
            P("sx", "sy", None, None),
            P("sx", "sy", None, None),
            P("sx", "sy", None),
            P("sx", None),
            P("sx", "sy", None, None),
        ),
        out_specs=P("sx", "sy", None, None),
        check_vma=False,
    )
```

```python
import functools

import jax
import jax.numpy as jnp
from jax import lax
from jax.experimental import pallas as pl
from jax.experimental.pallas import tpu as pltpu
from jax.sharding import PartitionSpec as P

MESH = pl.DeviceIdType.MESH
F32 = jnp.float32
BF16 = jnp.bfloat16
LANES = 128
OPPOSITE = (1, 0, 3, 2)


def down_rows(row):
    return jnp.broadcast_to(row, (LANES, LANES)).T


def kernel(
    n_sx, n_sy,
    res_hbm, w_hbm, blocks_hbm, pat_hbm, basis_hbm, inv_hbm, ord_hbm, sh_hbm,
    out,
    res, w_ref, basis, blocks, inv, ord_ref, sh_ref, pat_ref,
    wcol, weighted, acc, comb, onehot, inv_perm, pick,
    gath, csol, psol, face_out, basis_out, face_in, basis_in, psol_in,
    in_sem, blk_sem, row_s, near_s, pair_r, pv_r, cs_r, fb_r, fw_r, ps_r,
):
    i, j = lax.axis_index("sx"), lax.axis_index("sy")
    nb, knz, blk, _ = blocks.shape
    nprim = basis.shape[0]
    ncr = gath.shape[0]
    ni, nvec = res.shape
    face = ni // 4
    per = face // blk
    n_hub = n_sy // 2
    pair = 2 * nprim

    c, side = j // 2, lax.rem(j, 2)
    is_hub, is_leaf = side == 1, side == 0
    sibling = (i, j + 1 - 2 * side)

    loads = [
        pltpu.make_async_copy(source, target, in_sem.at[n])
        for n, (source, target) in enumerate(
            (
                (w_hbm, w_ref), (basis_hbm, basis), (res_hbm, res), (ord_hbm, ord_ref),
                (sh_hbm, sh_ref), (pat_hbm, pat_ref),
                (inv_hbm, inv.at[pl.ds(nprim, nprim)]),
            )
        )
    ]
    load_w, load_basis, load_res, load_ord, load_sh, load_pat, load_inv = loads
    load_blocks = [
        pltpu.make_async_copy(
            blocks_hbm.at[pl.ds(f * per, per)], blocks.at[pl.ds(f * per, per)], blk_sem.at[f]
        )
        for f in range(4)
    ]
    for copy in loads[:3]:
        copy.start()

    has = (i > 0, i < n_sx - 1, j > 0, j < n_sy - 1)
    there = ((i - 1, j), (i + 1, j), (i, j - 1), (i, j + 1))

    def hub_of(step):
        return lax.rem(c + step, n_hub)

    barrier = pltpu.get_barrier_semaphore()

    def signal(device):
        pl.semaphore_signal(barrier, inc=1, device_id=device, device_id_type=MESH)

    signal(sibling)

    def greet(step, carry):
        signal((i, 2 * hub_of(step) + 1))
        return carry

    lax.fori_loop(1, n_hub, greet, 0, unroll=n_hub <= 4)
    for f in (0, 1):

        @pl.when(has[f])
        def _():
            signal(there[f])

        @pl.when(jnp.logical_and(has[f], is_leaf))
        def _():
            signal((there[f][0], j + 1))

    @pl.when(is_hub)
    def _():
        def greet_leaf(step, carry):
            signal((i, 2 * hub_of(step)))
            return carry

        lax.fori_loop(1, n_hub, greet_leaf, 0, unroll=n_hub <= 4)

    for copy in load_blocks[:2] + [load_pat] + load_blocks[2:] + [load_inv, load_ord, load_sh]:
        copy.start()

    def remote(src, dst, send, recv, device):
        return pltpu.make_async_remote_copy(
            src_ref=src, dst_ref=dst, send_sem=send, recv_sem=recv,
            device_id=device, device_id_type=MESH,
        )

    def basis_copy(f):
        g = OPPOSITE[f]
        return remote(basis_out.at[f], basis_in.at[g], near_s.at[f], fb_r.at[g], there[f])

    def face_copy(f):
        g = OPPOSITE[f]
        return remote(face_out.at[f], face_in.at[g], near_s.at[f], fw_r.at[g], there[f])

    def inv_copy():
        return remote(
            inv_hbm, inv.at[pl.ds(0, nprim)], row_s.at[0], pair_r.at[0], sibling
        )

    def pv_copy(slot, hub):
        rows = pl.ds(pl.multiple_of(slot * nprim, nprim), nprim)
        return remote(
            gath.at[rows], gath.at[rows], row_s.at[0], pv_r.at[0], (i, 2 * hub + 1)
        )

    def csol_copy(slot, hub):
        rows = pl.ds(pl.multiple_of(slot * pair, pair), pair)
        return remote(
            csol.at[rows], csol.at[rows], row_s.at[0], cs_r.at[0], (i, 2 * hub + 1)
        )

    def pair_copy():
        rows = pl.ds(0, 3 * nprim)
        return remote(psol.at[rows], psol.at[rows], row_s.at[0], pair_r.at[0], sibling)

    def psol_copy(f, half):
        rows = pl.ds((1 + half) * nprim, nprim)
        return remote(
            psol.at[rows], psol_in.at[OPPOSITE[f]], near_s.at[f],
            ps_r.at[OPPOSITE[f]], (there[f][0], 2 * c + half),
        )

    def settle(ref, count, sem):
        part = ref.at[pl.ds(0, count)]
        pltpu.make_async_copy(part, part, sem).wait()

    for f in range(4):

        @pl.when(jnp.logical_not(has[f]))
        def _():
            face_in[f] = jnp.zeros(face_in.shape[1:], BF16)
            basis_in[f] = jnp.zeros(basis_in.shape[1:], BF16)
            if f < 2:
                psol_in[f] = jnp.zeros(psol_in.shape[1:], BF16)

    load_w.wait()
    load_basis.wait()
    for f in range(4):
        at = slice(f * face, (f + 1) * face)
        basis_out[f] = (w_ref[0:1, at] * basis[:, at].astype(F32)).astype(BF16)
    load_res.wait()
    pv = jnp.zeros((nprim, nvec), F32)
    for f in range(4):
        pv += jnp.dot(
            basis_out[f], res[f * face : (f + 1) * face, :], preferred_element_type=F32
        )
    own = pl.ds(pl.multiple_of(j * nprim, nprim), nprim)
    gath[own, :] = pv.astype(BF16)

    near = has[0].astype(jnp.int32) + has[1].astype(jnp.int32)
    pl.semaphore_wait(barrier, jnp.where(is_hub, n_sy - 1 + 2 * near, n_hub + near))

    @pl.when(is_leaf)
    def _():
        pv_copy(j, c).start()

    def send_pv(step, carry):
        pv_copy(j, hub_of(step)).start()
        return carry

    lax.fori_loop(1, n_hub, send_pv, 0, unroll=n_hub <= 4)

    @pl.when(is_leaf)
    def _():
        inv_copy().start()

    for f in range(4):

        @pl.when(has[f])
        def _():
            basis_copy(f).start()

    for b in range(nb):
        rows = slice(b * blk, (b + 1) * blk)
        wcol[b] = down_rows(w_ref[0:1, rows])
        weighted[b] = (wcol[b] * res[rows, :].astype(F32)).astype(BF16)

    load_pat.wait()
    for f in range(4):
        load_blocks[f].wait()
        for b in range(f * per, (f + 1) * per):
            left = jnp.concatenate([blocks[b, k] for k in range(knz)], axis=1)
            right = jnp.concatenate([weighted[pat_ref[k, b]] for k in range(knz)], axis=0)
            solved = wcol[b] * jnp.dot(left, right, preferred_element_type=F32)
            rows = slice(b * blk, (b + 1) * blk)
            acc[rows, :] = solved
            face_out[f, (b - f * per) * blk : (b - f * per + 1) * blk, :] = solved.astype(BF16)

        @pl.when(jnp.logical_and(has[f], is_leaf) if f == 3 else has[f])
        def _():
            face_copy(f).start()

    load_inv.wait()
    load_ord.wait()
    load_sh.wait()

    @pl.when(is_hub)
    def _():
        for m, who in enumerate((jnp.maximum(c - 1, 0), c, jnp.minimum(c + 1, n_hub - 1))):
            at = pl.ds(pl.multiple_of(who * LANES, LANES), LANES)
            col = down_rows(ord_ref[:, at].astype(F32))
            lane = lax.broadcasted_iota(jnp.int32, (LANES, LANES), 1).astype(F32)
            low = nprim if m == 0 else 0
            high = nprim if m == 2 else pair
            base = m * pair - nprim
            for q in range(ncr // LANES):
                hit = jnp.where(col == lane + float(q * LANES), 1.0, 0.0).astype(BF16)
                pick[base + low : base + high, q * LANES : (q + 1) * LANES] = hit[low:high, :]

        chunk = 512 if ncr <= 512 else LANES
        inv_copy().wait_recv()
        inv16 = inv[...].astype(BF16)

        def permute_columns(q, carry):
            at = pl.ds(pl.multiple_of(q * chunk, chunk), chunk)
            hit = lax.broadcasted_iota(jnp.int32, (ncr, chunk), 0) == ord_ref[:, at]
            inv_perm[:, at] = jnp.dot(
                inv16, jnp.where(hit, 1.0, 0.0).astype(BF16), preferred_element_type=F32
            ).astype(BF16)
            return carry

        lax.fori_loop(0, ncr // chunk, permute_columns, 0)

        settle(gath, (n_sy - 1) * nprim, pv_r.at[0])
        mine = pl.ds(pl.multiple_of(c * pair, pair), pair)
        csol[mine, :] = jnp.dot(
            inv_perm[...], gath[...], preferred_element_type=F32
        ).astype(BF16)

        def send_csol(step, carry):
            csol_copy(c, hub_of(step)).start()
            return carry

        lax.fori_loop(1, n_hub, send_csol, 0, unroll=n_hub <= 4)

        @pl.when(has[3])
        def _():
            face_copy(3).start()

    wide_lane = lax.broadcasted_iota(jnp.int32, (LANES, face), 1).astype(F32)
    for f in (2, 3, 0, 1):
        for q in range(face // LANES):
            at = slice(q * LANES, (q + 1) * LANES)
            col = down_rows(sh_ref[f : f + 1, at].astype(F32))
            col = jnp.concatenate([col] * (face // LANES), axis=1)
            onehot[f, at, :] = jnp.where(col == wide_lane, 1.0, 0.0).astype(BF16)

        @pl.when(has[f])
        def _():
            basis_copy(OPPOSITE[f]).wait_recv()

        moved = lax.dot_general(
            basis_in[f], onehot[f], (((1,), (1,)), ((), ())), preferred_element_type=F32
        )
        both = jnp.concatenate([basis_out[f].astype(F32), moved], axis=0)
        comb[f] = both.T.astype(BF16)

    @pl.when(is_hub)
    def _():
        settle(csol, (n_hub - 1) * pair, cs_r.at[0])
        psol[...] = jnp.dot(pick[...], csol[...], preferred_element_type=F32).astype(BF16)
        for half in (0, 1):
            for f in (0, 1):

                @pl.when(has[f])
                def _():
                    psol_copy(f, half).start()

        pair_copy().start()

    for f in (2, 3, 0, 1):

        @pl.when(has[f])
        def _():
            face_copy(OPPOSITE[f]).wait_recv()

        rows = slice(f * face, (f + 1) * face)
        acc[rows, :] = acc[rows, :] + jnp.dot(
            onehot[f], face_in[f], preferred_element_type=F32
        )

    @pl.when(is_leaf)
    def _():
        pair_copy().wait_recv()

    base = side * nprim

    def psol_rows(m):
        return psol[pl.ds(pl.multiple_of(base + m * nprim, nprim), nprim), :]

    for f in (2, 3, 0, 1):
        if f < 2:

            @pl.when(has[f])
            def _():
                psol_copy(OPPOSITE[f], 0).wait_recv()

        other = psol_in[f] if f < 2 else psol_rows(0 if f == 2 else 2)
        both = jnp.concatenate([psol_rows(1), other], axis=0)
        rows = slice(f * face, (f + 1) * face)
        out[rows, :] = (
            acc[rows, :]
            + jnp.dot(comb[f], both, preferred_element_type=F32)
        ).astype(BF16)

    settle(pick, 3 * nprim, row_s.at[0])
    sent = nprim * face // nvec + face
    for f in range(4):

        @pl.when(jnp.logical_and(has[f], is_hub))
        def _():
            settle(res, sent + (pair if f < 2 else 0), near_s.at[f])

        @pl.when(jnp.logical_and(has[f], is_leaf))
        def _():
            settle(res, sent, near_s.at[f])


def body(
    n_sx, n_sy,
    residual, weights, blocks, pattern, primal_basis, coarse_inverse, coarse_rows, shared_lists,
):
    ni, nvec = residual.shape[2:]
    nb, knz, blk = blocks.shape[2:5]
    nprim = primal_basis.shape[-1]
    ncr = coarse_rows.shape[-1]
    face = shared_lists.shape[-1]
    hbm = pl.BlockSpec(memory_space=pltpu.HBM)
    vmem = pl.BlockSpec(memory_space=pltpu.VMEM)
    dma = pltpu.SemaphoreType.DMA
    limit = 64 * 1024 * 1024 - 65536 - ni * nvec * 2
    total = pl.pallas_call(
        functools.partial(kernel, n_sx, n_sy),
        out_shape=pltpu.VMEM((ni, nvec), BF16),
        in_specs=[hbm] * 8,
        out_specs=vmem,
        scratch_shapes=[
            pltpu.VMEM((ni, nvec), BF16),
            pltpu.VMEM((1, ni), F32),
            pltpu.VMEM((nprim, ni), BF16),
            pltpu.VMEM((nb, knz, blk, blk), BF16),
            pltpu.VMEM((2 * nprim, ncr), F32),
            pltpu.VMEM((1, ncr), jnp.int32),
            pltpu.VMEM((4, face), jnp.int32),
            pltpu.SMEM((knz, nb), jnp.int32),
            pltpu.VMEM((nb, blk, LANES), F32),
            pltpu.VMEM((nb, blk, nvec), BF16),
            pltpu.VMEM((ni, nvec), F32),
            pltpu.VMEM((4, face, 2 * nprim), BF16),
            pltpu.VMEM((4, face, face), BF16),
            pltpu.VMEM((2 * nprim, ncr), BF16),
            pltpu.VMEM((4 * nprim, ncr), BF16),
            pltpu.VMEM((ncr, nvec), BF16),
            pltpu.VMEM((ncr, nvec), BF16),
            pltpu.VMEM((4 * nprim, nvec), BF16),
            pltpu.VMEM((4, face, nvec), BF16),
            pltpu.VMEM((4, nprim, face), BF16),
            pltpu.VMEM((4, face, nvec), BF16),
            pltpu.VMEM((4, nprim, face), BF16),
            pltpu.VMEM((2, nprim, nvec), BF16),
            dma((7,)), dma((4,)), dma((1,)), dma((4,)),
            dma((1,)), dma((1,)), dma((1,)), dma((4,)), dma((4,)), dma((2,)),
        ],
        compiler_params=pltpu.CompilerParams(
            collective_id=0, has_side_effects=True, vmem_limit_bytes=limit
        ),
    )(
        residual[0, 0], weights[0], blocks[0, 0], pattern[0, 0].T, primal_basis[0, 0].T,
        coarse_inverse[0], coarse_rows, shared_lists[0, 0],
    )
    pieces = 4

    def hand_over(held, target, sem):
        step = ni // pieces
        writes = [
            pltpu.make_async_copy(
                held.at[pl.ds(p * step, step)], target.at[pl.ds(p * step, step)], sem.at[p]
            )
            for p in range(pieces)
        ]
        for copy in writes:
            copy.start()
        for copy in writes:
            copy.wait()

    total = pl.pallas_call(
        hand_over,
        out_shape=jax.ShapeDtypeStruct((ni, nvec), BF16),
        in_specs=[vmem],
        out_specs=hbm,
        scratch_shapes=[dma((pieces,))],
        compiler_params=pltpu.CompilerParams(vmem_limit_bytes=4 * 1024 * 1024),
    )(total)
    return total[None, None]


def solution(mesh):
    return jax.shard_map(
        functools.partial(body, mesh.shape["sx"], mesh.shape["sy"]),
        mesh=mesh,
        in_specs=(
            P("sx", "sy", None, None),
            P("sx", "sy", None),
            P("sx", "sy", None, None, None, None),
            P("sx", "sy", None, None),
            P("sx", "sy", None, None),
            P("sx", "sy", None),
            P("sx", None),
            P("sx", "sy", None, None),
        ),
        out_specs=P("sx", "sy", None, None),
        check_vma=False,
    )
```

```python
import functools

import jax
import jax.numpy as jnp
from jax import lax
from jax.experimental import pallas as pl
from jax.experimental.pallas import tpu as pltpu
from jax.sharding import PartitionSpec as P

MESH = pl.DeviceIdType.MESH
F32 = jnp.float32
BF16 = jnp.bfloat16
LANES = 128
OPPOSITE = (1, 0, 3, 2)


def down_rows(row):
    return jnp.broadcast_to(row, (LANES, LANES)).T


def kernel(
    n_sx, n_sy,
    res_hbm, w_hbm, blocks_hbm, pat_hbm, basis_hbm, inv_hbm, ord_hbm, sh_hbm,
    out,
    res, w_ref, basis, blocks, inv, ord_ref, sh_ref, pat_ref,
    wcol, weighted, acc, comb, onehot, inv_perm, pick,
    gath, csol, psol, face_out, basis_out, face_in, basis_in, psol_in,
    corner_pick, corner_out, corner_in,
    in_sem, blk_sem, row_s, near_s, pair_r, pv_r, cs_r, fb_r, fw_r, ps_r, corner_s, corner_r,
):
    i, j = lax.axis_index("sx"), lax.axis_index("sy")
    nb, knz, blk, _ = blocks.shape
    nprim = basis.shape[0]
    ncr = gath.shape[0]
    ni, nvec = res.shape
    face = ni // 4
    per = face // blk
    n_hub = n_sy // 2
    pair = 2 * nprim

    c, side = j // 2, lax.rem(j, 2)
    is_hub, is_leaf = side == 1, side == 0
    sibling = (i, j + 1 - 2 * side)
    corner = jnp.logical_and(i == 0, c == 0)
    giver = jnp.logical_and(i == 1, is_hub)
    beside = jnp.logical_and(i == 1, c == 0)

    loads = [
        pltpu.make_async_copy(source, target, in_sem.at[n])
        for n, (source, target) in enumerate(
            (
                (w_hbm, w_ref), (basis_hbm, basis), (res_hbm, res), (ord_hbm, ord_ref),
                (sh_hbm, sh_ref), (pat_hbm, pat_ref),
                (inv_hbm, inv.at[pl.ds(nprim, nprim)]),
            )
        )
    ]
    load_w, load_basis, load_res, load_ord, load_sh, load_pat, load_inv = loads
    load_blocks = [
        pltpu.make_async_copy(
            blocks_hbm.at[pl.ds(f * per, per)], blocks.at[pl.ds(f * per, per)], blk_sem.at[f]
        )
        for f in range(4)
    ]
    for copy in loads[:3]:
        copy.start()

    has = (i > 0, i < n_sx - 1, j > 0, j < n_sy - 1)
    there = ((i - 1, j), (i + 1, j), (i, j - 1), (i, j + 1))

    def hub_of(step):
        return lax.rem(c + step, n_hub)

    barrier = pltpu.get_barrier_semaphore()

    def signal(device):
        pl.semaphore_signal(barrier, inc=1, device_id=device, device_id_type=MESH)

    signal(sibling)

    def greet(step, carry):
        signal((i, 2 * hub_of(step) + 1))
        return carry

    lax.fori_loop(1, n_hub, greet, 0, unroll=n_hub <= 4)
    for f in (0, 1):

        @pl.when(has[f])
        def _():
            signal(there[f])

        @pl.when(jnp.logical_and(has[f], is_leaf))
        def _():
            signal((there[f][0], j + 1))

    if n_sx > 1:

        @pl.when(corner)
        def _():
            def greet_giver(hub, carry):
                signal((1, 2 * hub + 1))
                return carry

            lax.fori_loop(1, n_hub, greet_giver, 0, unroll=n_hub <= 4)

    @pl.when(is_hub)
    def _():
        def greet_leaf(step, carry):
            signal((i, 2 * hub_of(step)))
            return carry

        lax.fori_loop(1, n_hub, greet_leaf, 0, unroll=n_hub <= 4)

    for copy in load_blocks[:2] + [load_pat] + load_blocks[2:] + [load_inv, load_ord, load_sh]:
        copy.start()

    def remote(src, dst, send, recv, device):
        return pltpu.make_async_remote_copy(
            src_ref=src, dst_ref=dst, send_sem=send, recv_sem=recv,
            device_id=device, device_id_type=MESH,
        )

    def basis_copy(f):
        g = OPPOSITE[f]
        return remote(basis_out.at[f], basis_in.at[g], near_s.at[f], fb_r.at[g], there[f])

    def face_copy(f):
        g = OPPOSITE[f]
        return remote(face_out.at[f], face_in.at[g], near_s.at[f], fw_r.at[g], there[f])

    def inv_copy():
        return remote(
            inv_hbm, inv.at[pl.ds(0, nprim)], row_s.at[0], pair_r.at[0], sibling
        )

    def pv_copy(slot, hub):
        rows = pl.ds(pl.multiple_of(slot * nprim, nprim), nprim)
        return remote(
            gath.at[rows], gath.at[rows], row_s.at[0], pv_r.at[0], (i, 2 * hub + 1)
        )

    def csol_copy(slot, hub):
        rows = pl.ds(pl.multiple_of(slot * pair, pair), pair)
        return remote(
            csol.at[rows], csol.at[rows], row_s.at[0], cs_r.at[0], (i, 2 * hub + 1)
        )

    def pair_copy():
        rows = pl.ds(0, 3 * nprim)
        return remote(psol.at[rows], psol.at[rows], row_s.at[0], pair_r.at[0], sibling)

    def psol_copy(f, half):
        rows = pl.ds((1 + half) * nprim, nprim)
        return remote(
            psol.at[rows], psol_in.at[OPPOSITE[f]], near_s.at[f],
            ps_r.at[OPPOSITE[f]], (there[f][0], 2 * c + half),
        )

    def corner_copy(half):
        source = pl.ds(half * nprim, nprim)
        target = pl.ds(pl.multiple_of(c * nprim, nprim), nprim)
        return remote(
            corner_out.at[source], corner_in.at[target], corner_s.at[0], corner_r.at[0],
            (0, half),
        )

    def settle(ref, count, sem):
        part = ref.at[pl.ds(0, count)]
        pltpu.make_async_copy(part, part, sem).wait()

    def sends(f):
        return jnp.logical_and(has[f], jnp.logical_not(beside)) if f == 0 else has[f]

    for f in range(4):

        @pl.when(jnp.logical_not(has[f]))
        def _():
            face_in[f] = jnp.zeros(face_in.shape[1:], BF16)
            basis_in[f] = jnp.zeros(basis_in.shape[1:], BF16)
            if f < 2:
                psol_in[f] = jnp.zeros(psol_in.shape[1:], BF16)

    load_w.wait()
    load_basis.wait()
    for f in range(4):
        at = slice(f * face, (f + 1) * face)
        basis_out[f] = (w_ref[0:1, at] * basis[:, at].astype(F32)).astype(BF16)
    load_res.wait()
    pv = jnp.zeros((nprim, nvec), F32)
    for f in range(4):
        pv += jnp.dot(
            basis_out[f], res[f * face : (f + 1) * face, :], preferred_element_type=F32
        )
    own = pl.ds(pl.multiple_of(j * nprim, nprim), nprim)
    gath[own, :] = pv.astype(BF16)

    near = has[0].astype(jnp.int32) + has[1].astype(jnp.int32)
    away = jnp.logical_and(i == 1, c > 0).astype(jnp.int32)
    pl.semaphore_wait(
        barrier, jnp.where(is_hub, n_sy - 1 + 2 * near + 2 * away, n_hub + near)
    )

    @pl.when(is_leaf)
    def _():
        pv_copy(j, c).start()

    def send_pv(step, carry):
        pv_copy(j, hub_of(step)).start()
        return carry

    lax.fori_loop(1, n_hub, send_pv, 0, unroll=n_hub <= 4)

    @pl.when(is_leaf)
    def _():
        inv_copy().start()

    for f in range(4):

        @pl.when(has[f])
        def _():
            basis_copy(f).start()

    for b in range(nb):
        rows = slice(b * blk, (b + 1) * blk)
        wcol[b] = down_rows(w_ref[0:1, rows])
        weighted[b] = (wcol[b] * res[rows, :].astype(F32)).astype(BF16)

    load_pat.wait()
    for f in range(4):
        load_blocks[f].wait()
        for b in range(f * per, (f + 1) * per):
            left = jnp.concatenate([blocks[b, k] for k in range(knz)], axis=1)
            right = jnp.concatenate([weighted[pat_ref[k, b]] for k in range(knz)], axis=0)
            solved = wcol[b] * jnp.dot(left, right, preferred_element_type=F32)
            rows = slice(b * blk, (b + 1) * blk)
            acc[rows, :] = solved
            face_out[f, (b - f * per) * blk : (b - f * per + 1) * blk, :] = solved.astype(BF16)

        @pl.when(jnp.logical_and(has[f], is_leaf) if f == 3 else has[f])
        def _():
            face_copy(f).start()

    load_inv.wait()
    load_ord.wait()
    load_sh.wait()

    @pl.when(is_hub)
    def _():
        for m, who in enumerate((jnp.maximum(c - 1, 0), c, jnp.minimum(c + 1, n_hub - 1))):
            at = pl.ds(pl.multiple_of(who * LANES, LANES), LANES)
            col = down_rows(ord_ref[:, at].astype(F32))
            lane = lax.broadcasted_iota(jnp.int32, (LANES, LANES), 1).astype(F32)
            low = nprim if m == 0 else 0
            high = nprim if m == 2 else pair
            base = m * pair - nprim
            for q in range(ncr // LANES):
                hit = jnp.where(col == lane + float(q * LANES), 1.0, 0.0).astype(BF16)
                pick[base + low : base + high, q * LANES : (q + 1) * LANES] = hit[low:high, :]

        col = down_rows(ord_ref[:, 0:LANES].astype(F32))
        row = lane + (c * pair).astype(F32)
        corner_pick[...] = jnp.where(col == row, 1.0, 0.0).astype(BF16)

        chunk = 512 if ncr <= 512 else LANES
        inv_copy().wait_recv()
        inv16 = inv[...].astype(BF16)

        def permute_columns(q, carry):
            at = pl.ds(pl.multiple_of(q * chunk, chunk), chunk)
            hit = lax.broadcasted_iota(jnp.int32, (ncr, chunk), 0) == ord_ref[:, at]
            inv_perm[:, at] = jnp.dot(
                inv16, jnp.where(hit, 1.0, 0.0).astype(BF16), preferred_element_type=F32
            ).astype(BF16)
            return carry

        lax.fori_loop(0, ncr // chunk, permute_columns, 0)

        settle(gath, (n_sy - 1) * nprim, pv_r.at[0])
        mine = pl.ds(pl.multiple_of(c * pair, pair), pair)
        csol[mine, :] = jnp.dot(
            inv_perm[...], gath[...], preferred_element_type=F32
        ).astype(BF16)

        def send_csol(step, carry):
            csol_copy(c, hub_of(step)).start()
            return carry

        lax.fori_loop(1, n_hub, send_csol, 0, unroll=n_hub <= 4)

        @pl.when(giver)
        def _():
            corner_out[...] = jnp.dot(
                corner_pick[...], csol[mine, :], preferred_element_type=F32
            ).astype(BF16)
            for half in (0, 1):
                corner_copy(half).start()

        @pl.when(has[3])
        def _():
            face_copy(3).start()

    wide_lane = lax.broadcasted_iota(jnp.int32, (LANES, face), 1).astype(F32)
    for f in (2, 3, 0, 1):
        for q in range(face // LANES):
            at = slice(q * LANES, (q + 1) * LANES)
            col = down_rows(sh_ref[f : f + 1, at].astype(F32))
            col = jnp.concatenate([col] * (face // LANES), axis=1)
            onehot[f, at, :] = jnp.where(col == wide_lane, 1.0, 0.0).astype(BF16)

        @pl.when(has[f])
        def _():
            basis_copy(OPPOSITE[f]).wait_recv()

        moved = lax.dot_general(
            basis_in[f], onehot[f], (((1,), (1,)), ((), ())), preferred_element_type=F32
        )
        both = jnp.concatenate([basis_out[f].astype(F32), moved], axis=0)
        comb[f] = both.T.astype(BF16)

    @pl.when(is_hub)
    def _():
        settle(csol, (n_hub - 1) * pair, cs_r.at[0])
        psol[...] = jnp.dot(pick[...], csol[...], preferred_element_type=F32).astype(BF16)
        for half in (0, 1):
            for f in (0, 1):

                @pl.when(sends(f))
                def _():
                    psol_copy(f, half).start()

        pair_copy().start()

    for f in (2, 3, 0, 1):

        @pl.when(has[f])
        def _():
            face_copy(OPPOSITE[f]).wait_recv()

        rows = slice(f * face, (f + 1) * face)
        acc[rows, :] = acc[rows, :] + jnp.dot(
            onehot[f], face_in[f], preferred_element_type=F32
        )

    @pl.when(is_leaf)
    def _():
        pair_copy().wait_recv()

    base = side * nprim

    def psol_rows(m):
        return psol[pl.ds(pl.multiple_of(base + m * nprim, nprim), nprim), :]

    for f in (2, 3, 0, 1):
        if f < 2:
            by_hub = jnp.logical_and(has[f], jnp.logical_not(corner)) if f == 1 else has[f]

            @pl.when(by_hub)
            def _():
                psol_copy(OPPOSITE[f], 0).wait_recv()

        if f == 1 and n_sx > 1:

            @pl.when(corner)
            def _():
                settle(corner_in, n_hub * nprim, corner_r.at[0])

                def add(hub, total):
                    rows = pl.ds(pl.multiple_of(hub * nprim, nprim), nprim)
                    return total + corner_in[rows, :].astype(F32)

                total = lax.fori_loop(
                    0, n_hub, add, jnp.zeros((nprim, nvec), F32), unroll=n_hub <= 4
                )
                psol_in[1] = total.astype(BF16)

        other = psol_in[f] if f < 2 else psol_rows(0 if f == 2 else 2)
        both = jnp.concatenate([psol_rows(1), other], axis=0)
        rows = slice(f * face, (f + 1) * face)
        out[rows, :] = (
            acc[rows, :]
            + jnp.dot(comb[f], both, preferred_element_type=F32)
        ).astype(BF16)

    settle(pick, 3 * nprim, row_s.at[0])
    sent = nprim * face // nvec + face
    for f in range(4):

        both = jnp.logical_and(sends(f), is_hub) if f < 2 else i < 0

        @pl.when(both)
        def _():
            settle(res, sent + pair, near_s.at[f])

        @pl.when(jnp.logical_and(has[f], jnp.logical_not(both)))
        def _():
            settle(res, sent, near_s.at[f])

    @pl.when(giver)
    def _():
        settle(corner_out, pair, corner_s.at[0])


def body(
    n_sx, n_sy,
    residual, weights, blocks, pattern, primal_basis, coarse_inverse, coarse_rows, shared_lists,
):
    ni, nvec = residual.shape[2:]
    nb, knz, blk = blocks.shape[2:5]
    nprim = primal_basis.shape[-1]
    ncr = coarse_rows.shape[-1]
    face = shared_lists.shape[-1]
    hbm = pl.BlockSpec(memory_space=pltpu.HBM)
    vmem = pl.BlockSpec(memory_space=pltpu.VMEM)
    dma = pltpu.SemaphoreType.DMA
    limit = 64 * 1024 * 1024 - 65536 - ni * nvec * 2
    total = pl.pallas_call(
        functools.partial(kernel, n_sx, n_sy),
        out_shape=pltpu.VMEM((ni, nvec), BF16),
        in_specs=[hbm] * 8,
        out_specs=vmem,
        scratch_shapes=[
            pltpu.VMEM((ni, nvec), BF16),
            pltpu.VMEM((1, ni), F32),
            pltpu.VMEM((nprim, ni), BF16),
            pltpu.VMEM((nb, knz, blk, blk), BF16),
            pltpu.VMEM((2 * nprim, ncr), F32),
            pltpu.VMEM((1, ncr), jnp.int32),
            pltpu.VMEM((4, face), jnp.int32),
            pltpu.SMEM((knz, nb), jnp.int32),
            pltpu.VMEM((nb, blk, LANES), F32),
            pltpu.VMEM((nb, blk, nvec), BF16),
            pltpu.VMEM((ni, nvec), F32),
            pltpu.VMEM((4, face, 2 * nprim), BF16),
            pltpu.VMEM((4, face, face), BF16),
            pltpu.VMEM((2 * nprim, ncr), BF16),
            pltpu.VMEM((4 * nprim, ncr), BF16),
            pltpu.VMEM((ncr, nvec), BF16),
            pltpu.VMEM((ncr, nvec), BF16),
            pltpu.VMEM((4 * nprim, nvec), BF16),
            pltpu.VMEM((4, face, nvec), BF16),
            pltpu.VMEM((4, nprim, face), BF16),
            pltpu.VMEM((4, face, nvec), BF16),
            pltpu.VMEM((4, nprim, face), BF16),
            pltpu.VMEM((2, nprim, nvec), BF16),
            pltpu.VMEM((2 * nprim, 2 * nprim), BF16),
            pltpu.VMEM((2 * nprim, nvec), BF16),
            pltpu.VMEM((n_sy // 2 * nprim, nvec), BF16),
            dma((7,)), dma((4,)), dma((1,)), dma((4,)),
            dma((1,)), dma((1,)), dma((1,)), dma((4,)), dma((4,)), dma((2,)), dma((1,)), dma((1,)),
        ],
        compiler_params=pltpu.CompilerParams(
            collective_id=0, has_side_effects=True, vmem_limit_bytes=limit
        ),
    )(
        residual[0, 0], weights[0], blocks[0, 0], pattern[0, 0].T, primal_basis[0, 0].T,
        coarse_inverse[0], coarse_rows, shared_lists[0, 0],
    )
    pieces = 4

    def hand_over(held, target, sem):
        step = ni // pieces
        writes = [
            pltpu.make_async_copy(
                held.at[pl.ds(p * step, step)], target.at[pl.ds(p * step, step)], sem.at[p]
            )
            for p in range(pieces)
        ]
        for copy in writes:
            copy.start()
        for copy in writes:
            copy.wait()

    total = pl.pallas_call(
        hand_over,
        out_shape=jax.ShapeDtypeStruct((ni, nvec), BF16),
        in_specs=[vmem],
        out_specs=hbm,
        scratch_shapes=[dma((pieces,))],
        compiler_params=pltpu.CompilerParams(vmem_limit_bytes=4 * 1024 * 1024),
    )(total)
    return total[None, None]


def solution(mesh):
    return jax.shard_map(
        functools.partial(body, mesh.shape["sx"], mesh.shape["sy"]),
        mesh=mesh,
        in_specs=(
            P("sx", "sy", None, None),
            P("sx", "sy", None),
            P("sx", "sy", None, None, None, None),
            P("sx", "sy", None, None),
            P("sx", "sy", None, None),
            P("sx", "sy", None),
            P("sx", None),
            P("sx", "sy", None, None),
        ),
        out_specs=P("sx", "sy", None, None),
        check_vma=False,
    )
```

```python
import functools

import jax
import jax.numpy as jnp
from jax import lax
from jax.experimental import pallas as pl
from jax.experimental.pallas import tpu as pltpu
from jax.sharding import PartitionSpec as P

MESH = pl.DeviceIdType.MESH
F32 = jnp.float32
BF16 = jnp.bfloat16
LANES = 128
OPPOSITE = (1, 0, 3, 2)


def down_rows(row):
    return jnp.broadcast_to(row, (LANES, LANES)).T


def kernel(
    n_sx, n_sy,
    res_hbm, w_hbm, blocks_hbm, pat_hbm, basis_hbm, inv_hbm, ord_hbm, sh_hbm,
    out,
    res, w_ref, basis, blocks, inv, ord_ref, sh_ref, pat_ref,
    wcol, weighted, acc, comb, onehot, inv_perm, pick,
    gath, csol, psol, face_out, basis_out, face_in, basis_in, psol_in,
    corner_pick, corner_out, corner_in,
    in_sem, blk_sem, row_s, near_s, pair_r, pv_r, cs_r, fb_r, fw_r, ps_r, corner_s, corner_r,
):
    i, j = lax.axis_index("sx"), lax.axis_index("sy")
    nb, knz, blk, _ = blocks.shape
    nprim = basis.shape[0]
    ncr = gath.shape[0]
    ni, nvec = res.shape
    face = ni // 4
    per = face // blk
    n_hub = n_sy // 2
    pair = 2 * nprim

    c, side = j // 2, lax.rem(j, 2)
    is_hub, is_leaf = side == 1, side == 0
    sibling = (i, j + 1 - 2 * side)
    corner = jnp.logical_and(i < n_sx - 1, c == 0)
    giver = jnp.logical_and(i > 0, is_hub)
    beside = jnp.logical_and(i > 0, c == 0)

    loads = [
        pltpu.make_async_copy(source, target, in_sem.at[n])
        for n, (source, target) in enumerate(
            (
                (w_hbm, w_ref), (basis_hbm, basis), (res_hbm, res), (ord_hbm, ord_ref),
                (sh_hbm, sh_ref), (pat_hbm, pat_ref),
                (inv_hbm, inv.at[pl.ds(nprim, nprim)]),
            )
        )
    ]
    load_w, load_basis, load_res, load_ord, load_sh, load_pat, load_inv = loads
    load_blocks = pltpu.make_async_copy(blocks_hbm, blocks, blk_sem.at[0])
    for copy in loads[:3]:
        copy.start()

    has = (i > 0, i < n_sx - 1, j > 0, j < n_sy - 1)
    there = ((i - 1, j), (i + 1, j), (i, j - 1), (i, j + 1))

    def hub_of(step):
        return lax.rem(c + step, n_hub)

    barrier = pltpu.get_barrier_semaphore()

    def signal(device):
        pl.semaphore_signal(barrier, inc=1, device_id=device, device_id_type=MESH)

    @pl.when(is_hub)
    def _():
        def greet_leaf(step, carry):
            signal((i, 2 * hub_of(step)))
            return carry

        lax.fori_loop(1, n_hub, greet_leaf, 0, unroll=n_hub <= 4)

    def greet(step, carry):
        signal((i, 2 * hub_of(step) + 1))
        return carry

    lax.fori_loop(1, n_hub, greet, 0, unroll=n_hub <= 4)
    signal(sibling)
    for f in (0, 1):

        @pl.when(has[f])
        def _():
            signal(there[f])

        @pl.when(jnp.logical_and(has[f], is_leaf))
        def _():
            signal((there[f][0], j + 1))

    if n_sx > 1:

        @pl.when(corner)
        def _():
            def greet_giver(hub, carry):
                signal((i + 1, 2 * hub + 1))
                return carry

            lax.fori_loop(1, n_hub, greet_giver, 0, unroll=n_hub <= 4)

    for copy in (load_blocks, load_pat, load_inv, load_ord, load_sh):
        copy.start()

    def remote(src, dst, send, recv, device):
        return pltpu.make_async_remote_copy(
            src_ref=src, dst_ref=dst, send_sem=send, recv_sem=recv,
            device_id=device, device_id_type=MESH,
        )

    def basis_copy(f):
        g = OPPOSITE[f]
        return remote(basis_out.at[f], basis_in.at[g], near_s.at[f // 2], fb_r.at[g // 2], there[f])

    def face_copy(f):
        g = OPPOSITE[f]
        return remote(face_out.at[f], face_in.at[g], near_s.at[f // 2], fw_r.at[g // 2], there[f])

    def inv_copy():
        return remote(
            inv_hbm, inv.at[pl.ds(0, nprim)], row_s.at[0], pair_r.at[0], sibling
        )

    def pv_copy(slot, hub):
        rows = pl.ds(pl.multiple_of(slot * nprim, nprim), nprim)
        return remote(
            gath.at[rows], gath.at[rows], row_s.at[0], pv_r.at[0], (i, 2 * hub + 1)
        )

    def csol_copy(slot, hub):
        rows = pl.ds(pl.multiple_of(slot * pair, pair), pair)
        return remote(
            csol.at[rows], csol.at[rows], row_s.at[0], cs_r.at[0], (i, 2 * hub + 1)
        )

    def pair_copy():
        rows = pl.ds(0, 3 * nprim)
        return remote(psol.at[rows], psol.at[rows], row_s.at[0], pair_r.at[0], sibling)

    def psol_copy(f, half):
        rows = pl.ds((1 + half) * nprim, nprim)
        return remote(
            psol.at[rows], psol_in.at[OPPOSITE[f]], near_s.at[0],
            ps_r.at[OPPOSITE[f]], (there[f][0], 2 * c + half),
        )

    def corner_copy(half):
        source = pl.ds(half * nprim, nprim)
        target = pl.ds(pl.multiple_of(c * nprim, nprim), nprim)
        return remote(
            corner_out.at[source], corner_in.at[target], corner_s.at[0], corner_r.at[0],
            (i - 1, half),
        )

    def settle(ref, count, sem):
        part = ref.at[pl.ds(0, count)]
        pltpu.make_async_copy(part, part, sem).wait()

    def settle_any(ref, counts, sem):
        for when, count in counts:

            @pl.when(when)
            def _():
                settle(ref, count, sem)

    both_z, one_z = jnp.logical_and(has[0], has[1]), has[0] != has[1]
    both_y, one_y = jnp.logical_and(has[2], has[3]), has[2] != has[3]

    def settle_near(ref, f, sem):
        both, one = ((both_z, one_z), (both_y, one_y))[f // 2]
        settle_any(ref, ((both, 2), (one, 1)), sem.at[f // 2])

    def sends(f):
        return jnp.logical_and(has[f], jnp.logical_not(beside)) if f == 0 else has[f]

    for f in range(4):

        @pl.when(jnp.logical_not(has[f]))
        def _():
            face_in[f] = jnp.zeros(face_in.shape[1:], BF16)
            basis_in[f] = jnp.zeros(basis_in.shape[1:], BF16)
            if f < 2:
                psol_in[f] = jnp.zeros(psol_in.shape[1:], BF16)

    load_w.wait()
    load_basis.wait()
    for f in range(4):
        at = slice(f * face, (f + 1) * face)
        basis_out[f] = (w_ref[0:1, at] * basis[:, at].astype(F32)).astype(BF16)
    load_res.wait()
    pv = jnp.zeros((nprim, nvec), F32)
    for f in range(4):
        pv += jnp.dot(
            basis_out[f], res[f * face : (f + 1) * face, :], preferred_element_type=F32
        )
    own = pl.ds(pl.multiple_of(j * nprim, nprim), nprim)
    gath[own, :] = pv.astype(BF16)

    near = has[0].astype(jnp.int32) + has[1].astype(jnp.int32)
    away = jnp.logical_and(i > 0, c > 0).astype(jnp.int32)
    pl.semaphore_wait(
        barrier, jnp.where(is_hub, n_sy - 1 + 2 * near + 2 * away, n_hub + near)
    )

    @pl.when(is_leaf)
    def _():
        pv_copy(j, c).start()

    def send_pv(step, carry):
        pv_copy(j, hub_of(step)).start()
        return carry

    lax.fori_loop(1, n_hub, send_pv, 0, unroll=n_hub <= 4)

    @pl.when(is_leaf)
    def _():
        inv_copy().start()

    for f in range(4):

        @pl.when(has[f])
        def _():
            basis_copy(f).start()

    for b in range(nb):
        rows = slice(b * blk, (b + 1) * blk)
        wcol[b] = down_rows(w_ref[0:1, rows])
        weighted[b] = (wcol[b] * res[rows, :].astype(F32)).astype(BF16)

    load_pat.wait()
    load_blocks.wait()
    for f in range(4):
        for b in range(f * per, (f + 1) * per):
            left = jnp.concatenate([blocks[b, k] for k in range(knz)], axis=1)
            right = jnp.concatenate([weighted[pat_ref[k, b]] for k in range(knz)], axis=0)
            solved = wcol[b] * jnp.dot(left, right, preferred_element_type=F32)
            rows = slice(b * blk, (b + 1) * blk)
            acc[rows, :] = solved
            face_out[f, (b - f * per) * blk : (b - f * per + 1) * blk, :] = solved.astype(BF16)

        @pl.when(jnp.logical_and(has[f], is_leaf) if f == 3 else has[f])
        def _():
            face_copy(f).start()

    load_inv.wait()
    load_ord.wait()
    load_sh.wait()

    @pl.when(is_hub)
    def _():
        for m, who in enumerate((jnp.maximum(c - 1, 0), c, jnp.minimum(c + 1, n_hub - 1))):
            at = pl.ds(pl.multiple_of(who * LANES, LANES), LANES)
            col = down_rows(ord_ref[:, at].astype(F32))
            lane = lax.broadcasted_iota(jnp.int32, (LANES, LANES), 1).astype(F32)
            low = nprim if m == 0 else 0
            high = nprim if m == 2 else pair
            base = m * pair - nprim
            for q in range(ncr // LANES):
                hit = jnp.where(col == lane + float(q * LANES), 1.0, 0.0).astype(BF16)
                pick[base + low : base + high, q * LANES : (q + 1) * LANES] = hit[low:high, :]

        col = down_rows(ord_ref[:, 0:LANES].astype(F32))
        row = lane + (c * pair).astype(F32)
        corner_pick[...] = jnp.where(col == row, 1.0, 0.0).astype(BF16)

        chunk = 512 if ncr <= 512 else LANES
        inv_copy().wait_recv()
        inv16 = inv[...].astype(BF16)

        def permute_columns(q, carry):
            at = pl.ds(pl.multiple_of(q * chunk, chunk), chunk)
            hit = lax.broadcasted_iota(jnp.int32, (ncr, chunk), 0) == ord_ref[:, at]
            inv_perm[:, at] = jnp.dot(
                inv16, jnp.where(hit, 1.0, 0.0).astype(BF16), preferred_element_type=F32
            ).astype(BF16)
            return carry

        lax.fori_loop(0, ncr // chunk, permute_columns, 0)

        settle(gath, (n_sy - 1) * nprim, pv_r.at[0])
        mine = pl.ds(pl.multiple_of(c * pair, pair), pair)
        csol[mine, :] = jnp.dot(
            inv_perm[...], gath[...], preferred_element_type=F32
        ).astype(BF16)

        def send_csol(step, carry):
            csol_copy(c, hub_of(step)).start()
            return carry

        lax.fori_loop(1, n_hub, send_csol, 0, unroll=n_hub <= 4)

        @pl.when(giver)
        def _():
            corner_out[...] = jnp.dot(
                corner_pick[...], csol[mine, :], preferred_element_type=F32
            ).astype(BF16)
            for half in (0, 1):
                corner_copy(half).start()

        @pl.when(has[3])
        def _():
            face_copy(3).start()

    wide_lane = lax.broadcasted_iota(jnp.int32, (LANES, face), 1).astype(F32)
    for f in (2, 3, 0, 1):
        for q in range(face // LANES):
            at = slice(q * LANES, (q + 1) * LANES)
            col = down_rows(sh_ref[f : f + 1, at].astype(F32))
            col = jnp.concatenate([col] * (face // LANES), axis=1)
            onehot[f, at, :] = jnp.where(col == wide_lane, 1.0, 0.0).astype(BF16)

        if f % 2 == 0:
            settle_near(basis_in, f, fb_r)

        moved = lax.dot_general(
            basis_in[f], onehot[f], (((1,), (1,)), ((), ())), preferred_element_type=F32
        )
        both = jnp.concatenate([basis_out[f].astype(F32), moved], axis=0)
        comb[f] = both.T.astype(BF16)

    @pl.when(is_hub)
    def _():
        settle(csol, (n_hub - 1) * pair, cs_r.at[0])
        psol[...] = jnp.dot(pick[...], csol[...], preferred_element_type=F32).astype(BF16)
        for half in (0, 1):
            for f in (0, 1):

                @pl.when(sends(f))
                def _():
                    psol_copy(f, half).start()

        pair_copy().start()

    for f in (2, 3, 0, 1):

        if f % 2 == 0:
            settle_near(face_in, f, fw_r)

        rows = slice(f * face, (f + 1) * face)
        acc[rows, :] = acc[rows, :] + jnp.dot(
            onehot[f], face_in[f], preferred_element_type=F32
        )

    @pl.when(is_leaf)
    def _():
        pair_copy().wait_recv()

    base = side * nprim

    def psol_rows(m):
        return psol[pl.ds(pl.multiple_of(base + m * nprim, nprim), nprim), :]

    for f in (2, 3, 0, 1):
        if f < 2:
            by_hub = jnp.logical_and(has[f], jnp.logical_not(corner)) if f == 1 else has[f]

            @pl.when(by_hub)
            def _():
                psol_copy(OPPOSITE[f], 0).wait_recv()

        if f == 1 and n_sx > 1:

            @pl.when(corner)
            def _():
                settle(corner_in, n_hub * nprim, corner_r.at[0])

                def add(hub, total):
                    rows = pl.ds(pl.multiple_of(hub * nprim, nprim), nprim)
                    return total + corner_in[rows, :].astype(F32)

                total = lax.fori_loop(
                    0, n_hub, add, jnp.zeros((nprim, nvec), F32), unroll=n_hub <= 4
                )
                psol_in[1] = total.astype(BF16)

        other = psol_in[f] if f < 2 else psol_rows(0 if f == 2 else 2)
        both = jnp.concatenate([psol_rows(1), other], axis=0)
        rows = slice(f * face, (f + 1) * face)
        out[rows, :] = (
            acc[rows, :]
            + jnp.dot(comb[f], both, preferred_element_type=F32)
        ).astype(BF16)

    settle(pick, 3 * nprim, row_s.at[0])
    sent = nprim * face // nvec + face
    settle_any(res, ((both_y, 2 * sent), (one_y, sent)), near_s.at[1])
    hub_z = jnp.logical_and(both_z, is_hub)
    settle_any(
        res,
        (
            (jnp.logical_and(hub_z, jnp.logical_not(beside)), 2 * (sent + pair)),
            (jnp.logical_and(hub_z, beside), 2 * sent + pair),
            (jnp.logical_and(one_z, jnp.logical_and(is_hub, sends(0) | has[1])), sent + pair),
            (jnp.logical_and(one_z, jnp.logical_and(is_hub, jnp.logical_not(sends(0) | has[1]))), sent),
            (jnp.logical_and(both_z, is_leaf), 2 * sent),
            (jnp.logical_and(one_z, is_leaf), sent),
        ),
        near_s.at[0],
    )

    @pl.when(giver)
    def _():
        settle(corner_out, pair, corner_s.at[0])


def body(
    n_sx, n_sy,
    residual, weights, blocks, pattern, primal_basis, coarse_inverse, coarse_rows, shared_lists,
):
    ni, nvec = residual.shape[2:]
    nb, knz, blk = blocks.shape[2:5]
    nprim = primal_basis.shape[-1]
    ncr = coarse_rows.shape[-1]
    face = shared_lists.shape[-1]
    hbm = pl.BlockSpec(memory_space=pltpu.HBM)
    vmem = pl.BlockSpec(memory_space=pltpu.VMEM)
    dma = pltpu.SemaphoreType.DMA
    limit = 64 * 1024 * 1024 - 65536 - ni * nvec * 2
    total = pl.pallas_call(
        functools.partial(kernel, n_sx, n_sy),
        out_shape=pltpu.VMEM((ni, nvec), BF16),
        in_specs=[hbm] * 8,
        out_specs=vmem,
        scratch_shapes=[
            pltpu.VMEM((ni, nvec), BF16),
            pltpu.VMEM((1, ni), F32),
            pltpu.VMEM((nprim, ni), BF16),
            pltpu.VMEM((nb, knz, blk, blk), BF16),
            pltpu.VMEM((2 * nprim, ncr), F32),
            pltpu.VMEM((1, ncr), jnp.int32),
            pltpu.VMEM((4, face), jnp.int32),
            pltpu.SMEM((knz, nb), jnp.int32),
            pltpu.VMEM((nb, blk, LANES), F32),
            pltpu.VMEM((nb, blk, nvec), BF16),
            pltpu.VMEM((ni, nvec), F32),
            pltpu.VMEM((4, face, 2 * nprim), BF16),
            pltpu.VMEM((4, face, face), BF16),
            pltpu.VMEM((2 * nprim, ncr), BF16),
            pltpu.VMEM((4 * nprim, ncr), BF16),
            pltpu.VMEM((ncr, nvec), BF16),
            pltpu.VMEM((ncr, nvec), BF16),
            pltpu.VMEM((4 * nprim, nvec), BF16),
            pltpu.VMEM((4, face, nvec), BF16),
            pltpu.VMEM((4, nprim, face), BF16),
            pltpu.VMEM((4, face, nvec), BF16),
            pltpu.VMEM((4, nprim, face), BF16),
            pltpu.VMEM((2, nprim, nvec), BF16),
            pltpu.VMEM((2 * nprim, 2 * nprim), BF16),
            pltpu.VMEM((2 * nprim, nvec), BF16),
            pltpu.VMEM((n_sy // 2 * nprim, nvec), BF16),
            dma((7,)), dma((1,)), dma((1,)), dma((2,)),
            dma((1,)), dma((1,)), dma((1,)), dma((2,)), dma((2,)), dma((2,)), dma((1,)), dma((1,)),
        ],
        compiler_params=pltpu.CompilerParams(
            collective_id=0, has_side_effects=True, vmem_limit_bytes=limit
        ),
    )(
        residual[0, 0], weights[0], blocks[0, 0], pattern[0, 0].T, primal_basis[0, 0].T,
        coarse_inverse[0], coarse_rows, shared_lists[0, 0],
    )
    pieces = 4

    def hand_over(held, target, sem):
        step = ni // pieces
        writes = [
            pltpu.make_async_copy(
                held.at[pl.ds(p * step, step)], target.at[pl.ds(p * step, step)], sem.at[0]
            )
            for p in range(pieces)
        ]
        for copy in writes:
            copy.start()
        pltpu.make_async_copy(held, target, sem.at[0]).wait()

    total = pl.pallas_call(
        hand_over,
        out_shape=jax.ShapeDtypeStruct((ni, nvec), BF16),
        in_specs=[vmem],
        out_specs=hbm,
        scratch_shapes=[dma((1,))],
        compiler_params=pltpu.CompilerParams(vmem_limit_bytes=4 * 1024 * 1024),
    )(total)
    return total[None, None]


def solution(mesh):
    return jax.shard_map(
        functools.partial(body, mesh.shape["sx"], mesh.shape["sy"]),
        mesh=mesh,
        in_specs=(
            P("sx", "sy", None, None),
            P("sx", "sy", None),
            P("sx", "sy", None, None, None, None),
            P("sx", "sy", None, None),
            P("sx", "sy", None, None),
            P("sx", "sy", None),
            P("sx", None),
            P("sx", "sy", None, None),
        ),
        out_specs=P("sx", "sy", None, None),
        check_vma=False,
    )
```

```python
import functools

import jax
import jax.numpy as jnp
from jax import lax
from jax.experimental import pallas as pl
from jax.experimental.pallas import tpu as pltpu
from jax.sharding import PartitionSpec as P

MESH = pl.DeviceIdType.MESH
F32 = jnp.float32
BF16 = jnp.bfloat16
LANES = 128
OPPOSITE = (1, 0, 3, 2)


def down_rows(row):
    return jnp.broadcast_to(row, (LANES, LANES)).T


def kernel(
    n_sx, n_sy,
    res_hbm, w_hbm, blocks_hbm, pat_hbm, basis_hbm, inv_hbm, ord_hbm, sh_hbm,
    out, acc_s, comb_s, psol_s,
    res, w_ref, basis, blocks, inv, ord_ref, sh_ref, pat_ref,
    wcol, weighted, acc, comb, onehot, inv_perm, pick,
    gath, csol, psol, face_out, basis_out, face_in, basis_in, psol_in,
    corner_pick, corner_out, corner_in,
    in_sem, blk_sem, row_s, near_s, pair_r, pv_r, cs_r, fb_r, fw_r, ps_r, corner_s, corner_r,
):
    i, j = lax.axis_index("sx"), lax.axis_index("sy")
    nb, knz, blk, _ = blocks.shape
    nprim = basis.shape[0]
    ncr = gath.shape[0]
    ni, nvec = res.shape
    face = ni // 4
    per = face // blk
    n_hub = n_sy // 2
    pair = 2 * nprim

    c, side = j // 2, lax.rem(j, 2)
    is_hub, is_leaf = side == 1, side == 0
    sibling = (i, j + 1 - 2 * side)
    corner = jnp.logical_and(i < n_sx - 1, c == 0)
    giver = jnp.logical_and(i > 0, is_hub)
    beside = jnp.logical_and(i > 0, c == 0)

    loads = [
        pltpu.make_async_copy(source, target, in_sem.at[n])
        for n, (source, target) in enumerate(
            (
                (w_hbm, w_ref), (basis_hbm, basis), (res_hbm, res), (ord_hbm, ord_ref),
                (sh_hbm, sh_ref), (pat_hbm, pat_ref),
                (inv_hbm, inv.at[pl.ds(nprim, nprim)]),
            )
        )
    ]
    load_w, load_basis, load_res, load_ord, load_sh, load_pat, load_inv = loads
    load_blocks = pltpu.make_async_copy(blocks_hbm, blocks, blk_sem.at[0])
    for copy in loads[:3]:
        copy.start()

    has = (i > 0, i < n_sx - 1, j > 0, j < n_sy - 1)
    there = ((i - 1, j), (i + 1, j), (i, j - 1), (i, j + 1))

    def hub_of(step):
        return lax.rem(c + step, n_hub)

    barrier = pltpu.get_barrier_semaphore()

    def signal(device):
        pl.semaphore_signal(barrier, inc=1, device_id=device, device_id_type=MESH)

    @pl.when(is_hub)
    def _():
        def greet_leaf(step, carry):
            signal((i, 2 * hub_of(step)))
            return carry

        lax.fori_loop(1, n_hub, greet_leaf, 0, unroll=n_hub <= 4)

    def greet(step, carry):
        signal((i, 2 * hub_of(step) + 1))
        return carry

    lax.fori_loop(1, n_hub, greet, 0, unroll=n_hub <= 4)
    signal(sibling)
    for f in (0, 1):

        @pl.when(has[f])
        def _():
            signal(there[f])

        @pl.when(jnp.logical_and(has[f], is_leaf))
        def _():
            signal((there[f][0], j + 1))

    if n_sx > 1:

        @pl.when(corner)
        def _():
            def greet_giver(hub, carry):
                signal((i + 1, 2 * hub + 1))
                return carry

            lax.fori_loop(1, n_hub, greet_giver, 0, unroll=n_hub <= 4)

    for copy in (load_blocks, load_pat, load_inv, load_ord, load_sh):
        copy.start()

    def remote(src, dst, send, recv, device):
        return pltpu.make_async_remote_copy(
            src_ref=src, dst_ref=dst, send_sem=send, recv_sem=recv,
            device_id=device, device_id_type=MESH,
        )

    def basis_copy(f):
        g = OPPOSITE[f]
        return remote(basis_out.at[f], basis_in.at[g], near_s.at[f // 2], fb_r.at[g // 2], there[f])

    def face_copy(f):
        g = OPPOSITE[f]
        return remote(face_out.at[f], face_in.at[g], near_s.at[f // 2], fw_r.at[g // 2], there[f])

    def inv_copy():
        return remote(
            inv_hbm, inv.at[pl.ds(0, nprim)], row_s.at[0], pair_r.at[0], sibling
        )

    def pv_copy(slot, hub):
        rows = pl.ds(pl.multiple_of(slot * nprim, nprim), nprim)
        return remote(
            gath.at[rows], gath.at[rows], row_s.at[0], pv_r.at[0], (i, 2 * hub + 1)
        )

    def csol_copy(slot, hub):
        rows = pl.ds(pl.multiple_of(slot * pair, pair), pair)
        return remote(
            csol.at[rows], csol.at[rows], row_s.at[0], cs_r.at[0], (i, 2 * hub + 1)
        )

    def pair_copy():
        rows = pl.ds(0, 3 * nprim)
        return remote(psol.at[rows], psol.at[rows], row_s.at[0], pair_r.at[0], sibling)

    def psol_copy(f, half):
        rows = pl.ds((1 + half) * nprim, nprim)
        return remote(
            psol.at[rows], psol_in.at[OPPOSITE[f]], near_s.at[0],
            ps_r.at[OPPOSITE[f]], (there[f][0], 2 * c + half),
        )

    def corner_copy(half):
        source = pl.ds(half * nprim, nprim)
        target = pl.ds(pl.multiple_of(c * nprim, nprim), nprim)
        return remote(
            corner_out.at[source], corner_in.at[target], corner_s.at[0], corner_r.at[0],
            (i - 1, half),
        )

    def settle(ref, count, sem):
        part = ref.at[pl.ds(0, count)]
        pltpu.make_async_copy(part, part, sem).wait()

    def settle_any(ref, counts, sem):
        for when, count in counts:

            @pl.when(when)
            def _():
                settle(ref, count, sem)

    both_z, one_z = jnp.logical_and(has[0], has[1]), has[0] != has[1]
    both_y, one_y = jnp.logical_and(has[2], has[3]), has[2] != has[3]

    def settle_near(ref, f, sem):
        both, one = ((both_z, one_z), (both_y, one_y))[f // 2]
        settle_any(ref, ((both, 2), (one, 1)), sem.at[f // 2])

    def sends(f):
        return jnp.logical_and(has[f], jnp.logical_not(beside)) if f == 0 else has[f]

    for f in range(4):

        @pl.when(jnp.logical_not(has[f]))
        def _():
            face_in[f] = jnp.zeros(face_in.shape[1:], BF16)
            basis_in[f] = jnp.zeros(basis_in.shape[1:], BF16)
            if f < 2:
                psol_in[f] = jnp.zeros(psol_in.shape[1:], BF16)

    load_w.wait()
    load_basis.wait()
    for f in range(4):
        at = slice(f * face, (f + 1) * face)
        basis_out[f] = (w_ref[0:1, at] * basis[:, at].astype(F32)).astype(BF16)
    load_res.wait()
    pv = jnp.zeros((nprim, nvec), F32)
    for f in range(4):
        pv += jnp.dot(
            basis_out[f], res[f * face : (f + 1) * face, :], preferred_element_type=F32
        )
    own = pl.ds(pl.multiple_of(j * nprim, nprim), nprim)
    gath[own, :] = pv.astype(BF16)

    near = has[0].astype(jnp.int32) + has[1].astype(jnp.int32)
    away = jnp.logical_and(i > 0, c > 0).astype(jnp.int32)
    pl.semaphore_wait(
        barrier, jnp.where(is_hub, n_sy - 1 + 2 * near + 2 * away, n_hub + near)
    )

    @pl.when(is_leaf)
    def _():
        pv_copy(j, c).start()

    def send_pv(step, carry):
        pv_copy(j, hub_of(step)).start()
        return carry

    lax.fori_loop(1, n_hub, send_pv, 0, unroll=n_hub <= 4)

    @pl.when(is_leaf)
    def _():
        inv_copy().start()

    for f in range(4):

        @pl.when(has[f])
        def _():
            basis_copy(f).start()

    for b in range(nb):
        rows = slice(b * blk, (b + 1) * blk)
        wcol[b] = down_rows(w_ref[0:1, rows])
        weighted[b] = (wcol[b] * res[rows, :].astype(F32)).astype(BF16)

    load_pat.wait()
    load_blocks.wait()
    for f in range(4):
        for b in range(f * per, (f + 1) * per):
            left = jnp.concatenate([blocks[b, k] for k in range(knz)], axis=1)
            right = jnp.concatenate([weighted[pat_ref[k, b]] for k in range(knz)], axis=0)
            solved = wcol[b] * jnp.dot(left, right, preferred_element_type=F32)
            rows = slice(b * blk, (b + 1) * blk)
            acc[rows, :] = solved
            face_out[f, (b - f * per) * blk : (b - f * per + 1) * blk, :] = solved.astype(BF16)

        @pl.when(jnp.logical_and(has[f], is_leaf) if f == 3 else has[f])
        def _():
            face_copy(f).start()

    load_inv.wait()
    load_ord.wait()
    load_sh.wait()

    @pl.when(is_hub)
    def _():
        for m, who in enumerate((jnp.maximum(c - 1, 0), c, jnp.minimum(c + 1, n_hub - 1))):
            at = pl.ds(pl.multiple_of(who * LANES, LANES), LANES)
            col = down_rows(ord_ref[:, at].astype(F32))
            lane = lax.broadcasted_iota(jnp.int32, (LANES, LANES), 1).astype(F32)
            low = nprim if m == 0 else 0
            high = nprim if m == 2 else pair
            base = m * pair - nprim
            for q in range(ncr // LANES):
                hit = jnp.where(col == lane + float(q * LANES), 1.0, 0.0).astype(BF16)
                pick[base + low : base + high, q * LANES : (q + 1) * LANES] = hit[low:high, :]

        col = down_rows(ord_ref[:, 0:LANES].astype(F32))
        row = lane + (c * pair).astype(F32)
        corner_pick[...] = jnp.where(col == row, 1.0, 0.0).astype(BF16)

        chunk = 512 if ncr <= 512 else LANES
        inv_copy().wait_recv()
        inv16 = inv[...].astype(BF16)

        def permute_columns(q, carry):
            at = pl.ds(pl.multiple_of(q * chunk, chunk), chunk)
            hit = lax.broadcasted_iota(jnp.int32, (ncr, chunk), 0) == ord_ref[:, at]
            inv_perm[:, at] = jnp.dot(
                inv16, jnp.where(hit, 1.0, 0.0).astype(BF16), preferred_element_type=F32
            ).astype(BF16)
            return carry

        lax.fori_loop(0, ncr // chunk, permute_columns, 0)

        settle(gath, (n_sy - 1) * nprim, pv_r.at[0])
        mine = pl.ds(pl.multiple_of(c * pair, pair), pair)
        csol[mine, :] = jnp.dot(
            inv_perm[...], gath[...], preferred_element_type=F32
        ).astype(BF16)

        def send_csol(step, carry):
            csol_copy(c, hub_of(step)).start()
            return carry

        lax.fori_loop(1, n_hub, send_csol, 0, unroll=n_hub <= 4)

        @pl.when(giver)
        def _():
            corner_out[...] = jnp.dot(
                corner_pick[...], csol[mine, :], preferred_element_type=F32
            ).astype(BF16)
            for half in (0, 1):
                corner_copy(half).start()

        @pl.when(has[3])
        def _():
            face_copy(3).start()

    wide_lane = lax.broadcasted_iota(jnp.int32, (LANES, face), 1).astype(F32)
    for f in (2, 3, 0, 1):
        for q in range(face // LANES):
            at = slice(q * LANES, (q + 1) * LANES)
            col = down_rows(sh_ref[f : f + 1, at].astype(F32))
            col = jnp.concatenate([col] * (face // LANES), axis=1)
            onehot[f, at, :] = jnp.where(col == wide_lane, 1.0, 0.0).astype(BF16)

        if f % 2 == 0:
            settle_near(basis_in, f, fb_r)

        moved = lax.dot_general(
            basis_in[f], onehot[f], (((1,), (1,)), ((), ())), preferred_element_type=F32
        )
        both = jnp.concatenate([basis_out[f].astype(F32), moved], axis=0)
        mixed = both.T.astype(BF16)
        if f == 1:
            comb_s[...] = mixed
        else:
            comb[f] = mixed

    @pl.when(is_hub)
    def _():
        settle(csol, (n_hub - 1) * pair, cs_r.at[0])
        psol[...] = jnp.dot(pick[...], csol[...], preferred_element_type=F32).astype(BF16)
        for half in (0, 1):
            for f in (0, 1):

                @pl.when(sends(f))
                def _():
                    psol_copy(f, half).start()

        pair_copy().start()

    for f in (2, 3, 0, 1):

        if f % 2 == 0:
            settle_near(face_in, f, fw_r)

        rows = slice(f * face, (f + 1) * face)
        summed = acc[rows, :] + jnp.dot(
            onehot[f], face_in[f], preferred_element_type=F32
        )
        if f == 1:
            acc_s[...] = summed
        else:
            acc[rows, :] = summed

    @pl.when(is_leaf)
    def _():
        pair_copy().wait_recv()

    base = side * nprim

    def psol_rows(m):
        return psol[pl.ds(pl.multiple_of(base + m * nprim, nprim), nprim), :]

    for f in (2, 3, 0, 1):
        if f < 2:
            by_hub = jnp.logical_and(has[f], jnp.logical_not(corner)) if f == 1 else has[f]

            @pl.when(by_hub)
            def _():
                psol_copy(OPPOSITE[f], 0).wait_recv()

        if f == 1 and n_sx > 1:

            @pl.when(corner)
            def _():
                settle(corner_in, n_hub * nprim, corner_r.at[0])

                def add(hub, total):
                    rows = pl.ds(pl.multiple_of(hub * nprim, nprim), nprim)
                    return total + corner_in[rows, :].astype(F32)

                total = lax.fori_loop(
                    0, n_hub, add, jnp.zeros((nprim, nvec), F32), unroll=n_hub <= 4
                )
                psol_in[1] = total.astype(BF16)

        other = psol_in[f] if f < 2 else psol_rows(0 if f == 2 else 2)
        both = jnp.concatenate([psol_rows(1), other], axis=0)
        if f == 1:
            psol_s[...] = both
        else:
            rows = slice(f * face, (f + 1) * face)
            out[rows, :] = (
                acc[rows, :]
                + jnp.dot(comb[f], both, preferred_element_type=F32)
            ).astype(BF16)

    settle(pick, 3 * nprim, row_s.at[0])
    sent = nprim * face // nvec + face
    settle_any(res, ((both_y, 2 * sent), (one_y, sent)), near_s.at[1])
    hub_z = jnp.logical_and(both_z, is_hub)
    settle_any(
        res,
        (
            (jnp.logical_and(hub_z, jnp.logical_not(beside)), 2 * (sent + pair)),
            (jnp.logical_and(hub_z, beside), 2 * sent + pair),
            (jnp.logical_and(one_z, jnp.logical_and(is_hub, sends(0) | has[1])), sent + pair),
            (jnp.logical_and(one_z, jnp.logical_and(is_hub, jnp.logical_not(sends(0) | has[1]))), sent),
            (jnp.logical_and(both_z, is_leaf), 2 * sent),
            (jnp.logical_and(one_z, is_leaf), sent),
        ),
        near_s.at[0],
    )

    @pl.when(giver)
    def _():
        settle(corner_out, pair, corner_s.at[0])


def body(
    n_sx, n_sy,
    residual, weights, blocks, pattern, primal_basis, coarse_inverse, coarse_rows, shared_lists,
):
    ni, nvec = residual.shape[2:]
    nb, knz, blk = blocks.shape[2:5]
    nprim = primal_basis.shape[-1]
    ncr = coarse_rows.shape[-1]
    face = shared_lists.shape[-1]
    hbm = pl.BlockSpec(memory_space=pltpu.HBM)
    vmem = pl.BlockSpec(memory_space=pltpu.VMEM)
    dma = pltpu.SemaphoreType.DMA
    pair = 2 * nprim
    held_bytes = ni * nvec * 2 + face * nvec * 4 + face * pair * 2 + pair * nvec * 2
    limit = 64 * 1024 * 1024 - 65536 - held_bytes
    held = pl.pallas_call(
        functools.partial(kernel, n_sx, n_sy),
        out_shape=(
            pltpu.VMEM((ni, nvec), BF16),
            pltpu.VMEM((face, nvec), F32),
            pltpu.VMEM((face, pair), BF16),
            pltpu.VMEM((pair, nvec), BF16),
        ),
        in_specs=[hbm] * 8,
        out_specs=(vmem,) * 4,
        scratch_shapes=[
            pltpu.VMEM((ni, nvec), BF16),
            pltpu.VMEM((1, ni), F32),
            pltpu.VMEM((nprim, ni), BF16),
            pltpu.VMEM((nb, knz, blk, blk), BF16),
            pltpu.VMEM((2 * nprim, ncr), F32),
            pltpu.VMEM((1, ncr), jnp.int32),
            pltpu.VMEM((4, face), jnp.int32),
            pltpu.SMEM((knz, nb), jnp.int32),
            pltpu.VMEM((nb, blk, LANES), F32),
            pltpu.VMEM((nb, blk, nvec), BF16),
            pltpu.VMEM((ni, nvec), F32),
            pltpu.VMEM((4, face, 2 * nprim), BF16),
            pltpu.VMEM((4, face, face), BF16),
            pltpu.VMEM((2 * nprim, ncr), BF16),
            pltpu.VMEM((4 * nprim, ncr), BF16),
            pltpu.VMEM((ncr, nvec), BF16),
            pltpu.VMEM((ncr, nvec), BF16),
            pltpu.VMEM((4 * nprim, nvec), BF16),
            pltpu.VMEM((4, face, nvec), BF16),
            pltpu.VMEM((4, nprim, face), BF16),
            pltpu.VMEM((4, face, nvec), BF16),
            pltpu.VMEM((4, nprim, face), BF16),
            pltpu.VMEM((2, nprim, nvec), BF16),
            pltpu.VMEM((2 * nprim, 2 * nprim), BF16),
            pltpu.VMEM((2 * nprim, nvec), BF16),
            pltpu.VMEM((n_sy // 2 * nprim, nvec), BF16),
            dma((7,)), dma((1,)), dma((1,)), dma((2,)),
            dma((1,)), dma((1,)), dma((1,)), dma((2,)), dma((2,)), dma((2,)), dma((1,)), dma((1,)),
        ],
        compiler_params=pltpu.CompilerParams(
            collective_id=0, has_side_effects=True, vmem_limit_bytes=limit
        ),
    )(
        residual[0, 0], weights[0], blocks[0, 0], pattern[0, 0].T, primal_basis[0, 0].T,
        coarse_inverse[0], coarse_rows, shared_lists[0, 0],
    )

    def hand_over(held, acc_s, comb_s, psol_s, target, south, sem):
        rest = pl.ds(2 * face, 2 * face)
        parts = [(held, pl.ds(0, face)), (held, rest)]
        for source, at in parts:
            pltpu.make_async_copy(source.at[at], target.at[at], sem.at[0]).start()
        south[...] = (
            acc_s[...] + jnp.dot(comb_s[...], psol_s[...], preferred_element_type=F32)
        ).astype(BF16)
        pltpu.make_async_copy(south, target.at[pl.ds(face, face)], sem.at[0]).start()
        pltpu.make_async_copy(held, target, sem.at[0]).wait()

    total = pl.pallas_call(
        hand_over,
        out_shape=jax.ShapeDtypeStruct((ni, nvec), BF16),
        in_specs=[vmem] * 4,
        out_specs=hbm,
        scratch_shapes=[pltpu.VMEM((face, nvec), BF16), dma((1,))],
        compiler_params=pltpu.CompilerParams(vmem_limit_bytes=4 * 1024 * 1024),
    )(*held)
    return total[None, None]


def solution(mesh):
    return jax.shard_map(
        functools.partial(body, mesh.shape["sx"], mesh.shape["sy"]),
        mesh=mesh,
        in_specs=(
            P("sx", "sy", None, None),
            P("sx", "sy", None),
            P("sx", "sy", None, None, None, None),
            P("sx", "sy", None, None),
            P("sx", "sy", None, None),
            P("sx", "sy", None),
            P("sx", None),
            P("sx", "sy", None, None),
        ),
        out_specs=P("sx", "sy", None, None),
        check_vma=False,
    )
```

```python
import functools

import jax
import jax.numpy as jnp
from jax import lax
from jax.experimental import pallas as pl
from jax.experimental.pallas import tpu as pltpu
from jax.sharding import PartitionSpec as P

MESH = pl.DeviceIdType.MESH
F32 = jnp.float32
BF16 = jnp.bfloat16
LANES = 128
OPPOSITE = (1, 0, 3, 2)


def down_rows(row):
    return jnp.broadcast_to(row, (LANES, LANES)).T


def kernel(
    n_sx, n_sy,
    res_hbm, w_hbm, blocks_hbm, pat_hbm, basis_hbm, inv_hbm, ord_hbm, sh_hbm,
    out, acc_s, comb_s, psol_s,
    res, w_ref, basis, blocks, inv, ord_ref, sh_ref, pat_ref,
    wcol, weighted, acc, comb, onehot, inv_perm, pick,
    gath, csol, psol, face_out, basis_out, face_in, basis_in, psol_in,
    corner_pick, corner_out, corner_in,
    in_sem, blk_sem, row_s, near_s, pair_r, pv_r, cs_r, fb_r, fw_r, ps_r, corner_s, corner_r,
):
    i, j = lax.axis_index("sx"), lax.axis_index("sy")
    nb, knz, blk, _ = blocks.shape
    nprim = basis.shape[0]
    ncr = gath.shape[0]
    ni, nvec = res.shape
    face = ni // 4
    per = face // blk
    n_hub = n_sy // 2
    pair = 2 * nprim

    c, side = j // 2, lax.rem(j, 2)
    is_hub, is_leaf = side == 1, side == 0
    sibling = (i, j + 1 - 2 * side)
    corner = jnp.logical_and(i < n_sx - 1, c == 0)
    giver = jnp.logical_and(i > 0, is_hub)
    beside = jnp.logical_and(i > 0, c == 0)

    loads = [
        pltpu.make_async_copy(source, target, in_sem.at[n])
        for n, (source, target) in enumerate(
            (
                (w_hbm, w_ref), (basis_hbm, basis), (res_hbm, res), (ord_hbm, ord_ref),
                (sh_hbm, sh_ref), (pat_hbm, pat_ref),
                (inv_hbm, inv.at[pl.ds(nprim, nprim)]),
            )
        )
    ]
    load_w, load_basis, load_res, load_ord, load_sh, load_pat, load_inv = loads
    load_blocks = pltpu.make_async_copy(blocks_hbm, blocks, blk_sem.at[0])
    for copy in loads[:3]:
        copy.start()

    has = (i > 0, i < n_sx - 1, j > 0, j < n_sy - 1)
    there = ((i - 1, j), (i + 1, j), (i, j - 1), (i, j + 1))

    def hub_of(step):
        return lax.rem(c + step, n_hub)

    barrier = pltpu.get_barrier_semaphore()

    def signal(device):
        pl.semaphore_signal(barrier, inc=1, device_id=device, device_id_type=MESH)

    @pl.when(is_hub)
    def _():
        def greet_leaf(step, carry):
            signal((i, 2 * hub_of(step)))
            return carry

        lax.fori_loop(1, n_hub, greet_leaf, 0, unroll=n_hub <= 4)

    def greet(step, carry):
        signal((i, 2 * hub_of(step) + 1))
        return carry

    lax.fori_loop(1, n_hub, greet, 0, unroll=n_hub <= 4)
    signal(sibling)
    for f in (0, 1):

        @pl.when(has[f])
        def _():
            signal(there[f])

        @pl.when(jnp.logical_and(has[f], is_leaf))
        def _():
            signal((there[f][0], j + 1))

    if n_sx > 1:

        @pl.when(corner)
        def _():
            def greet_giver(hub, carry):
                signal((i + 1, 2 * hub + 1))
                return carry

            lax.fori_loop(1, n_hub, greet_giver, 0, unroll=n_hub <= 4)

    for copy in (load_blocks, load_pat, load_inv, load_ord, load_sh):
        copy.start()

    def remote(src, dst, send, recv, device):
        return pltpu.make_async_remote_copy(
            src_ref=src, dst_ref=dst, send_sem=send, recv_sem=recv,
            device_id=device, device_id_type=MESH,
        )

    def basis_copy(f):
        g = OPPOSITE[f]
        return remote(basis_out.at[f], basis_in.at[g], near_s.at[f // 2], fb_r.at[g // 2], there[f])

    def face_copy(f):
        g = OPPOSITE[f]
        return remote(face_out.at[f], face_in.at[g], near_s.at[f // 2], fw_r.at[g // 2], there[f])

    def inv_copy():
        return remote(
            inv_hbm, inv.at[pl.ds(0, nprim)], row_s.at[0], pair_r.at[0], sibling
        )

    def pv_copy(slot, hub):
        rows = pl.ds(pl.multiple_of(slot * nprim, nprim), nprim)
        return remote(
            gath.at[rows], gath.at[rows], row_s.at[0], pv_r.at[0], (i, 2 * hub + 1)
        )

    def csol_copy(slot, hub):
        rows = pl.ds(pl.multiple_of(slot * pair, pair), pair)
        return remote(
            csol.at[rows], csol.at[rows], row_s.at[0], cs_r.at[0], (i, 2 * hub + 1)
        )

    def pair_copy():
        rows = pl.ds(0, 3 * nprim)
        return remote(psol.at[rows], psol.at[rows], row_s.at[0], pair_r.at[0], sibling)

    def psol_copy(f, half):
        rows = pl.ds((1 + half) * nprim, nprim)
        return remote(
            psol.at[rows], psol_in.at[OPPOSITE[f]], near_s.at[0],
            ps_r.at[OPPOSITE[f]], (there[f][0], 2 * c + half),
        )

    def corner_copy(half):
        source = pl.ds(half * nprim, nprim)
        target = pl.ds(pl.multiple_of(c * nprim, nprim), nprim)
        return remote(
            corner_out.at[source], corner_in.at[target], corner_s.at[0], corner_r.at[0],
            (i - 1, half),
        )

    def settle(ref, count, sem):
        part = ref.at[pl.ds(0, count)]
        pltpu.make_async_copy(part, part, sem).wait()

    def settle_any(ref, counts, sem):
        for when, count in counts:

            @pl.when(when)
            def _():
                settle(ref, count, sem)

    both_z, one_z = jnp.logical_and(has[0], has[1]), has[0] != has[1]
    both_y, one_y = jnp.logical_and(has[2], has[3]), has[2] != has[3]

    def settle_near(ref, f, sem):
        both, one = ((both_z, one_z), (both_y, one_y))[f // 2]
        settle_any(ref, ((both, 2), (one, 1)), sem.at[f // 2])

    def sends(f):
        return jnp.logical_and(has[f], jnp.logical_not(beside)) if f == 0 else has[f]

    for f in range(4):

        @pl.when(jnp.logical_not(has[f]))
        def _():
            face_in[f] = jnp.zeros(face_in.shape[1:], BF16)
            basis_in[f] = jnp.zeros(basis_in.shape[1:], BF16)
            if f < 2:
                psol_in[f] = jnp.zeros(psol_in.shape[1:], BF16)

    load_w.wait()
    load_basis.wait()
    for f in range(4):
        at = slice(f * face, (f + 1) * face)
        basis_out[f] = (w_ref[0:1, at] * basis[:, at].astype(F32)).astype(BF16)
    load_res.wait()
    pv = jnp.zeros((nprim, nvec), F32)
    for f in range(4):
        pv += jnp.dot(
            basis_out[f], res[f * face : (f + 1) * face, :], preferred_element_type=F32
        )
    own = pl.ds(pl.multiple_of(j * nprim, nprim), nprim)
    gath[own, :] = pv.astype(BF16)

    near = has[0].astype(jnp.int32) + has[1].astype(jnp.int32)
    away = jnp.logical_and(i > 0, c > 0).astype(jnp.int32)
    pl.semaphore_wait(
        barrier, jnp.where(is_hub, n_sy - 1 + 2 * near + 2 * away, n_hub + near)
    )

    @pl.when(is_leaf)
    def _():
        pv_copy(j, c).start()

    def send_pv(step, carry):
        pv_copy(j, hub_of(step)).start()
        return carry

    lax.fori_loop(1, n_hub, send_pv, 0, unroll=n_hub <= 4)

    @pl.when(is_leaf)
    def _():
        inv_copy().start()

    for f in range(4):

        @pl.when(has[f])
        def _():
            basis_copy(f).start()

    for b in range(nb):
        rows = slice(b * blk, (b + 1) * blk)
        wcol[b] = down_rows(w_ref[0:1, rows])
        weighted[b] = (wcol[b] * res[rows, :].astype(F32)).astype(BF16)

    load_pat.wait()
    load_blocks.wait()
    for f in range(4):
        for b in range(f * per, (f + 1) * per):
            left = jnp.concatenate([blocks[b, k] for k in range(knz)], axis=1)
            right = jnp.concatenate([weighted[pat_ref[k, b]] for k in range(knz)], axis=0)
            solved = wcol[b] * jnp.dot(left, right, preferred_element_type=F32)
            rows = slice(b * blk, (b + 1) * blk)
            acc[rows, :] = solved
            face_out[f, (b - f * per) * blk : (b - f * per + 1) * blk, :] = solved.astype(BF16)

        @pl.when(jnp.logical_and(has[f], is_leaf) if f == 3 else has[f])
        def _():
            face_copy(f).start()

    load_inv.wait()
    load_ord.wait()
    load_sh.wait()

    @pl.when(is_hub)
    def _():
        for m, who in enumerate((jnp.maximum(c - 1, 0), c, jnp.minimum(c + 1, n_hub - 1))):
            at = pl.ds(pl.multiple_of(who * LANES, LANES), LANES)
            col = down_rows(ord_ref[:, at].astype(F32))
            lane = lax.broadcasted_iota(jnp.int32, (LANES, LANES), 1).astype(F32)
            low = nprim if m == 0 else 0
            high = nprim if m == 2 else pair
            base = m * pair - nprim
            for q in range(ncr // LANES):
                hit = jnp.where(col == lane + float(q * LANES), 1.0, 0.0).astype(BF16)
                pick[base + low : base + high, q * LANES : (q + 1) * LANES] = hit[low:high, :]

        col = down_rows(ord_ref[:, 0:LANES].astype(F32))
        row = lane + (c * pair).astype(F32)
        corner_pick[...] = jnp.where(col == row, 1.0, 0.0).astype(BF16)

        chunk = 512 if ncr <= 512 else LANES
        inv_copy().wait_recv()
        inv16 = inv[...].astype(BF16)

        def permute_columns(q, carry):
            at = pl.ds(pl.multiple_of(q * chunk, chunk), chunk)
            hit = lax.broadcasted_iota(jnp.int32, (ncr, chunk), 0) == ord_ref[:, at]
            inv_perm[:, at] = jnp.dot(
                inv16, jnp.where(hit, 1.0, 0.0).astype(BF16), preferred_element_type=F32
            ).astype(BF16)
            return carry

        lax.fori_loop(0, ncr // chunk, permute_columns, 0)

        settle(gath, (n_sy - 1) * nprim, pv_r.at[0])
        mine = pl.ds(pl.multiple_of(c * pair, pair), pair)
        csol[mine, :] = jnp.dot(
            inv_perm[...], gath[...], preferred_element_type=F32
        ).astype(BF16)

        def send_csol(step, carry):
            csol_copy(c, hub_of(step)).start()
            return carry

        lax.fori_loop(1, n_hub, send_csol, 0, unroll=n_hub <= 4)

        @pl.when(giver)
        def _():
            corner_out[...] = jnp.dot(
                corner_pick[...], csol[mine, :], preferred_element_type=F32
            ).astype(BF16)
            for half in (0, 1):
                corner_copy(half).start()

        @pl.when(has[3])
        def _():
            face_copy(3).start()

    wide_lane = lax.broadcasted_iota(jnp.int32, (LANES, face), 1).astype(F32)
    for f in (2, 3, 0, 1):
        for q in range(face // LANES):
            at = slice(q * LANES, (q + 1) * LANES)
            col = down_rows(sh_ref[f : f + 1, at].astype(F32))
            col = jnp.concatenate([col] * (face // LANES), axis=1)
            onehot[f, at, :] = jnp.where(col == wide_lane, 1.0, 0.0).astype(BF16)

        if f % 2 == 0:
            settle_near(basis_in, f, fb_r)

        moved = lax.dot_general(
            basis_in[f], onehot[f], (((1,), (1,)), ((), ())), preferred_element_type=F32
        )
        both = jnp.concatenate([basis_out[f].astype(F32), moved], axis=0)
        mixed = both.T.astype(BF16)
        if f == 1:
            comb_s[...] = mixed
        else:
            comb[f] = mixed

    @pl.when(is_hub)
    def _():
        settle(csol, (n_hub - 1) * pair, cs_r.at[0])
        sent_on = slice(0, 3 * nprim)
        psol[sent_on, :] = jnp.dot(
            pick[sent_on, :], csol[...], preferred_element_type=F32
        ).astype(BF16)
        pair_copy().start()
        for half in (0, 1):
            for f in (0, 1):

                @pl.when(sends(f))
                def _():
                    psol_copy(f, half).start()

        kept = slice(3 * nprim, 4 * nprim)
        psol[kept, :] = jnp.dot(
            pick[kept, :], csol[...], preferred_element_type=F32
        ).astype(BF16)

    for f in (2, 3, 0, 1):

        if f % 2 == 0:
            settle_near(face_in, f, fw_r)

        rows = slice(f * face, (f + 1) * face)
        summed = acc[rows, :] + jnp.dot(
            onehot[f], face_in[f], preferred_element_type=F32
        )
        if f == 1:
            acc_s[...] = summed
        else:
            acc[rows, :] = summed

    @pl.when(is_leaf)
    def _():
        pair_copy().wait_recv()

    base = side * nprim

    def psol_rows(m):
        return psol[pl.ds(pl.multiple_of(base + m * nprim, nprim), nprim), :]

    for f in (2, 3, 0, 1):
        if f < 2:
            by_hub = jnp.logical_and(has[f], jnp.logical_not(corner)) if f == 1 else has[f]

            @pl.when(by_hub)
            def _():
                psol_copy(OPPOSITE[f], 0).wait_recv()

        if f == 1 and n_sx > 1:

            @pl.when(corner)
            def _():
                settle(corner_in, n_hub * nprim, corner_r.at[0])

                def add(hub, total):
                    rows = pl.ds(pl.multiple_of(hub * nprim, nprim), nprim)
                    return total + corner_in[rows, :].astype(F32)

                total = lax.fori_loop(
                    0, n_hub, add, jnp.zeros((nprim, nvec), F32), unroll=n_hub <= 4
                )
                psol_in[1] = total.astype(BF16)

        other = psol_in[f] if f < 2 else psol_rows(0 if f == 2 else 2)
        both = jnp.concatenate([psol_rows(1), other], axis=0)
        if f == 1:
            psol_s[...] = both
        else:
            rows = slice(f * face, (f + 1) * face)
            out[rows, :] = (
                acc[rows, :]
                + jnp.dot(comb[f], both, preferred_element_type=F32)
            ).astype(BF16)

    settle(pick, 3 * nprim, row_s.at[0])
    sent = nprim * face // nvec + face
    settle_any(res, ((both_y, 2 * sent), (one_y, sent)), near_s.at[1])
    hub_z = jnp.logical_and(both_z, is_hub)
    settle_any(
        res,
        (
            (jnp.logical_and(hub_z, jnp.logical_not(beside)), 2 * (sent + pair)),
            (jnp.logical_and(hub_z, beside), 2 * sent + pair),
            (jnp.logical_and(one_z, jnp.logical_and(is_hub, sends(0) | has[1])), sent + pair),
            (jnp.logical_and(one_z, jnp.logical_and(is_hub, jnp.logical_not(sends(0) | has[1]))), sent),
            (jnp.logical_and(both_z, is_leaf), 2 * sent),
            (jnp.logical_and(one_z, is_leaf), sent),
        ),
        near_s.at[0],
    )

    @pl.when(giver)
    def _():
        settle(corner_out, pair, corner_s.at[0])


def body(
    n_sx, n_sy,
    residual, weights, blocks, pattern, primal_basis, coarse_inverse, coarse_rows, shared_lists,
):
    ni, nvec = residual.shape[2:]
    nb, knz, blk = blocks.shape[2:5]
    nprim = primal_basis.shape[-1]
    ncr = coarse_rows.shape[-1]
    face = shared_lists.shape[-1]
    hbm = pl.BlockSpec(memory_space=pltpu.HBM)
    vmem = pl.BlockSpec(memory_space=pltpu.VMEM)
    dma = pltpu.SemaphoreType.DMA
    pair = 2 * nprim
    held_bytes = ni * nvec * 2 + face * nvec * 4 + face * pair * 2 + pair * nvec * 2
    limit = 64 * 1024 * 1024 - 65536 - held_bytes
    held = pl.pallas_call(
        functools.partial(kernel, n_sx, n_sy),
        out_shape=(
            pltpu.VMEM((ni, nvec), BF16),
            pltpu.VMEM((face, nvec), F32),
            pltpu.VMEM((face, pair), BF16),
            pltpu.VMEM((pair, nvec), BF16),
        ),
        in_specs=[hbm] * 8,
        out_specs=(vmem,) * 4,
        scratch_shapes=[
            pltpu.VMEM((ni, nvec), BF16),
            pltpu.VMEM((1, ni), F32),
            pltpu.VMEM((nprim, ni), BF16),
            pltpu.VMEM((nb, knz, blk, blk), BF16),
            pltpu.VMEM((2 * nprim, ncr), F32),
            pltpu.VMEM((1, ncr), jnp.int32),
            pltpu.VMEM((4, face), jnp.int32),
            pltpu.SMEM((knz, nb), jnp.int32),
            pltpu.VMEM((nb, blk, LANES), F32),
            pltpu.VMEM((nb, blk, nvec), BF16),
            pltpu.VMEM((ni, nvec), F32),
            pltpu.VMEM((4, face, 2 * nprim), BF16),
            pltpu.VMEM((4, face, face), BF16),
            pltpu.VMEM((2 * nprim, ncr), BF16),
            pltpu.VMEM((4 * nprim, ncr), BF16),
            pltpu.VMEM((ncr, nvec), BF16),
            pltpu.VMEM((ncr, nvec), BF16),
            pltpu.VMEM((4 * nprim, nvec), BF16),
            pltpu.VMEM((4, face, nvec), BF16),
            pltpu.VMEM((4, nprim, face), BF16),
            pltpu.VMEM((4, face, nvec), BF16),
            pltpu.VMEM((4, nprim, face), BF16),
            pltpu.VMEM((2, nprim, nvec), BF16),
            pltpu.VMEM((2 * nprim, 2 * nprim), BF16),
            pltpu.VMEM((2 * nprim, nvec), BF16),
            pltpu.VMEM((n_sy // 2 * nprim, nvec), BF16),
            dma((7,)), dma((1,)), dma((1,)), dma((2,)),
            dma((1,)), dma((1,)), dma((1,)), dma((2,)), dma((2,)), dma((2,)), dma((1,)), dma((1,)),
        ],
        compiler_params=pltpu.CompilerParams(
            collective_id=0, has_side_effects=True, vmem_limit_bytes=limit
        ),
    )(
        residual[0, 0], weights[0], blocks[0, 0], pattern[0, 0].T, primal_basis[0, 0].T,
        coarse_inverse[0], coarse_rows, shared_lists[0, 0],
    )

    def hand_over(held, acc_s, comb_s, psol_s, target, south, sem):
        rest = pl.ds(2 * face, 2 * face)
        parts = [(held, pl.ds(0, face)), (held, rest)]
        for source, at in parts:
            pltpu.make_async_copy(source.at[at], target.at[at], sem.at[0]).start()
        south[...] = (
            acc_s[...] + jnp.dot(comb_s[...], psol_s[...], preferred_element_type=F32)
        ).astype(BF16)
        pltpu.make_async_copy(south, target.at[pl.ds(face, face)], sem.at[0]).start()
        pltpu.make_async_copy(held, target, sem.at[0]).wait()

    total = pl.pallas_call(
        hand_over,
        out_shape=jax.ShapeDtypeStruct((ni, nvec), BF16),
        in_specs=[vmem] * 4,
        out_specs=hbm,
        scratch_shapes=[pltpu.VMEM((face, nvec), BF16), dma((1,))],
        compiler_params=pltpu.CompilerParams(vmem_limit_bytes=4 * 1024 * 1024),
    )(*held)
    return total[None, None]


def solution(mesh):
    return jax.shard_map(
        functools.partial(body, mesh.shape["sx"], mesh.shape["sy"]),
        mesh=mesh,
        in_specs=(
            P("sx", "sy", None, None),
            P("sx", "sy", None),
            P("sx", "sy", None, None, None, None),
            P("sx", "sy", None, None),
            P("sx", "sy", None, None),
            P("sx", "sy", None),
            P("sx", None),
            P("sx", "sy", None, None),
        ),
        out_specs=P("sx", "sy", None, None),
        check_vma=False,
    )
```

```python
import functools

import jax
import jax.numpy as jnp
from jax import lax
from jax.experimental import pallas as pl
from jax.experimental.pallas import tpu as pltpu
from jax.sharding import PartitionSpec as P

MESH = pl.DeviceIdType.MESH
F32 = jnp.float32
BF16 = jnp.bfloat16
LANES = 128
OPPOSITE = (1, 0, 3, 2)


def down_rows(row):
    return jnp.broadcast_to(row, (LANES, LANES)).T


def kernel(
    n_sx, n_sy,
    res_hbm, w_hbm, blocks_hbm, pat_hbm, basis_hbm, inv_hbm, ord_hbm, sh_hbm,
    out, acc_s, comb_s, psol_s,
    res, w_ref, basis, blocks, inv, ord_ref, sh_ref, pat_ref,
    wcol, weighted, acc, comb, onehot, inv_perm, pick,
    gath, csol, psol, face_out, basis_out, face_in, basis_in, psol_in,
    corner_pick, corner_out, corner_in,
    in_sem, blk_sem, row_s, near_s, pair_r, pv_r, cs_r, fb_r, fw_r, ps_r, corner_s, corner_r,
):
    i, j = lax.axis_index("sx"), lax.axis_index("sy")
    nb, knz, blk, _ = blocks.shape
    nprim = basis.shape[0]
    ncr = gath.shape[0]
    ni, nvec = res.shape
    face = ni // 4
    per = face // blk
    n_hub = n_sy // 2
    pair = 2 * nprim

    c, side = j // 2, lax.rem(j, 2)
    is_hub, is_leaf = side == 1, side == 0
    sibling = (i, j + 1 - 2 * side)
    corner = jnp.logical_and(i < n_sx - 1, c == 0)
    giver = jnp.logical_and(i > 0, is_hub)
    beside = jnp.logical_and(i > 0, c == 0)

    loads = [
        pltpu.make_async_copy(source, target, in_sem.at[n])
        for n, (source, target) in enumerate(
            (
                (w_hbm, w_ref), (basis_hbm, basis), (res_hbm, res), (ord_hbm, ord_ref),
                (sh_hbm, sh_ref), (pat_hbm, pat_ref),
                (inv_hbm, inv.at[pl.ds(nprim, nprim)]),
            )
        )
    ]
    load_w, load_basis, load_res, load_ord, load_sh, load_pat, load_inv = loads
    load_blocks = pltpu.make_async_copy(blocks_hbm, blocks, blk_sem.at[0])
    for copy in loads[:3]:
        copy.start()

    has = (i > 0, i < n_sx - 1, j > 0, j < n_sy - 1)
    there = ((i - 1, j), (i + 1, j), (i, j - 1), (i, j + 1))

    def hub_of(step):
        return lax.rem(c + step, n_hub)

    barrier = pltpu.get_barrier_semaphore()

    def signal(device):
        pl.semaphore_signal(barrier, inc=1, device_id=device, device_id_type=MESH)

    @pl.when(is_hub)
    def _():
        def greet_leaf(step, carry):
            signal((i, 2 * hub_of(step)))
            return carry

        lax.fori_loop(1, n_hub, greet_leaf, 0, unroll=n_hub <= 4)

    def greet(step, carry):
        signal((i, 2 * hub_of(step) + 1))
        return carry

    lax.fori_loop(1, n_hub, greet, 0, unroll=n_hub <= 4)
    signal(sibling)
    for f in (0, 1):

        @pl.when(has[f])
        def _():
            signal(there[f])

        @pl.when(jnp.logical_and(has[f], is_leaf))
        def _():
            signal((there[f][0], j + 1))

    if n_sx > 1:

        @pl.when(corner)
        def _():
            def greet_giver(hub, carry):
                signal((i + 1, 2 * hub + 1))
                return carry

            lax.fori_loop(1, n_hub, greet_giver, 0, unroll=n_hub <= 4)

    for copy in (load_blocks, load_pat, load_inv, load_ord, load_sh):
        copy.start()

    def remote(src, dst, send, recv, device):
        return pltpu.make_async_remote_copy(
            src_ref=src, dst_ref=dst, send_sem=send, recv_sem=recv,
            device_id=device, device_id_type=MESH,
        )

    def basis_copy(f):
        g = OPPOSITE[f]
        return remote(basis_out.at[f], basis_in.at[g], near_s.at[f // 2], fb_r.at[g // 2], there[f])

    def face_copy(f):
        g = OPPOSITE[f]
        return remote(face_out.at[f], face_in.at[g], near_s.at[f // 2], fw_r.at[g // 2], there[f])

    def inv_copy():
        return remote(
            inv_hbm, inv.at[pl.ds(0, nprim)], row_s.at[0], pair_r.at[0], sibling
        )

    def pv_copy(slot, hub):
        rows = pl.ds(pl.multiple_of(slot * nprim, nprim), nprim)
        return remote(
            gath.at[rows], gath.at[rows], row_s.at[0], pv_r.at[0], (i, 2 * hub + 1)
        )

    def csol_copy(slot, hub):
        rows = pl.ds(pl.multiple_of(slot * pair, pair), pair)
        return remote(
            csol.at[rows], csol.at[rows], row_s.at[0], cs_r.at[0], (i, 2 * hub + 1)
        )

    def pair_copy():
        rows = pl.ds(0, 3 * nprim)
        return remote(psol.at[rows], psol.at[rows], row_s.at[0], pair_r.at[0], sibling)

    def psol_copy(f, half):
        rows = pl.ds((1 + half) * nprim, nprim)
        return remote(
            psol.at[rows], psol_in.at[OPPOSITE[f]], near_s.at[0],
            ps_r.at[OPPOSITE[f]], (there[f][0], 2 * c + half),
        )

    def corner_copy(half):
        source = pl.ds(half * nprim, nprim)
        target = pl.ds(pl.multiple_of(c * nprim, nprim), nprim)
        return remote(
            corner_out.at[source], corner_in.at[target], corner_s.at[0], corner_r.at[0],
            (i - 1, half),
        )

    def settle(ref, count, sem):
        part = ref.at[pl.ds(0, count)]
        pltpu.make_async_copy(part, part, sem).wait()

    def settle_any(ref, counts, sem):
        for when, count in counts:

            @pl.when(when)
            def _():
                settle(ref, count, sem)

    both_z, one_z = jnp.logical_and(has[0], has[1]), has[0] != has[1]
    both_y, one_y = jnp.logical_and(has[2], has[3]), has[2] != has[3]

    def settle_near(ref, f, sem):
        both, one = ((both_z, one_z), (both_y, one_y))[f // 2]
        settle_any(ref, ((both, 2), (one, 1)), sem.at[f // 2])

    def sends(f):
        return jnp.logical_and(has[f], jnp.logical_not(beside)) if f == 0 else has[f]

    for f in range(4):

        @pl.when(jnp.logical_not(has[f]))
        def _():
            face_in[f] = jnp.zeros(face_in.shape[1:], BF16)
            basis_in[f] = jnp.zeros(basis_in.shape[1:], BF16)
            if f < 2:
                psol_in[f] = jnp.zeros(psol_in.shape[1:], BF16)

    load_w.wait()
    load_basis.wait()
    for f in range(4):
        at = slice(f * face, (f + 1) * face)
        basis_out[f] = (w_ref[0:1, at] * basis[:, at].astype(F32)).astype(BF16)
    load_res.wait()
    pv = jnp.zeros((nprim, nvec), F32)
    for f in range(4):
        pv += jnp.dot(
            basis_out[f], res[f * face : (f + 1) * face, :], preferred_element_type=F32
        )
    own = pl.ds(pl.multiple_of(j * nprim, nprim), nprim)
    gath[own, :] = pv.astype(BF16)

    near = has[0].astype(jnp.int32) + has[1].astype(jnp.int32)
    away = jnp.logical_and(i > 0, c > 0).astype(jnp.int32)
    pl.semaphore_wait(
        barrier, jnp.where(is_hub, n_sy - 1 + 2 * near + 2 * away, n_hub + near)
    )

    @pl.when(is_leaf)
    def _():
        pv_copy(j, c).start()

    def send_pv(step, carry):
        pv_copy(j, hub_of(step)).start()
        return carry

    lax.fori_loop(1, n_hub, send_pv, 0, unroll=n_hub <= 4)

    @pl.when(is_leaf)
    def _():
        inv_copy().start()

    for f in range(4):

        @pl.when(has[f])
        def _():
            basis_copy(f).start()

    for b in range(nb):
        rows = slice(b * blk, (b + 1) * blk)
        wcol[b] = down_rows(w_ref[0:1, rows])
        weighted[b] = (wcol[b] * res[rows, :].astype(F32)).astype(BF16)

    load_pat.wait()
    load_blocks.wait()
    for f in range(4):
        for b in range(f * per, (f + 1) * per):
            left = jnp.concatenate([blocks[b, k] for k in range(knz)], axis=1)
            right = jnp.concatenate([weighted[pat_ref[k, b]] for k in range(knz)], axis=0)
            solved = wcol[b] * jnp.dot(left, right, preferred_element_type=F32)
            rows = slice(b * blk, (b + 1) * blk)
            acc[rows, :] = solved
            face_out[f, (b - f * per) * blk : (b - f * per + 1) * blk, :] = solved.astype(BF16)

        @pl.when(jnp.logical_and(has[f], is_leaf) if f == 3 else has[f])
        def _():
            face_copy(f).start()

    load_inv.wait()
    load_ord.wait()
    load_sh.wait()

    @pl.when(is_hub)
    def _():
        for m, who in enumerate((jnp.maximum(c - 1, 0), c, jnp.minimum(c + 1, n_hub - 1))):
            at = pl.ds(pl.multiple_of(who * LANES, LANES), LANES)
            col = down_rows(ord_ref[:, at].astype(F32))
            lane = lax.broadcasted_iota(jnp.int32, (LANES, LANES), 1).astype(F32)
            low = nprim if m == 0 else 0
            high = nprim if m == 2 else pair
            base = m * pair - nprim
            for q in range(ncr // LANES):
                hit = jnp.where(col == lane + float(q * LANES), 1.0, 0.0).astype(BF16)
                pick[base + low : base + high, q * LANES : (q + 1) * LANES] = hit[low:high, :]

        col = down_rows(ord_ref[:, 0:LANES].astype(F32))
        row = lane + (c * pair).astype(F32)
        corner_pick[...] = jnp.where(col == row, 1.0, 0.0).astype(BF16)

        chunk = 512 if ncr <= 512 else LANES
        inv_copy().wait_recv()
        inv16 = inv[...].astype(BF16)

        def permute_columns(q, carry):
            at = pl.ds(pl.multiple_of(q * chunk, chunk), chunk)
            hit = lax.broadcasted_iota(jnp.int32, (ncr, chunk), 0) == ord_ref[:, at]
            inv_perm[:, at] = jnp.dot(
                inv16, jnp.where(hit, 1.0, 0.0).astype(BF16), preferred_element_type=F32
            ).astype(BF16)
            return carry

        lax.fori_loop(0, ncr // chunk, permute_columns, 0)

        settle(gath, (n_sy - 1) * nprim, pv_r.at[0])
        mine = pl.ds(pl.multiple_of(c * pair, pair), pair)
        csol[mine, :] = jnp.dot(
            inv_perm[...], gath[...], preferred_element_type=F32
        ).astype(BF16)

        def send_csol(step, carry):
            csol_copy(c, hub_of(step)).start()
            return carry

        lax.fori_loop(1, n_hub, send_csol, 0, unroll=n_hub <= 4)

        @pl.when(giver)
        def _():
            corner_out[...] = jnp.dot(
                corner_pick[...], csol[mine, :], preferred_element_type=F32
            ).astype(BF16)
            for half in (0, 1):
                corner_copy(half).start()

        @pl.when(has[3])
        def _():
            face_copy(3).start()

    wide_lane = lax.broadcasted_iota(jnp.int32, (LANES, face), 1).astype(F32)
    for f in (2, 3, 0, 1):
        for q in range(face // LANES):
            at = slice(q * LANES, (q + 1) * LANES)
            col = down_rows(sh_ref[f : f + 1, at].astype(F32))
            col = jnp.concatenate([col] * (face // LANES), axis=1)
            onehot[f, at, :] = jnp.where(col == wide_lane, 1.0, 0.0).astype(BF16)

        if f % 2 == 0:
            settle_near(basis_in, f, fb_r)

        moved = lax.dot_general(
            basis_in[f], onehot[f], (((1,), (1,)), ((), ())), preferred_element_type=F32
        )
        both = jnp.concatenate([basis_out[f].astype(F32), moved], axis=0)
        mixed = both.T.astype(BF16)
        if f == 1:
            comb_s[...] = mixed
        else:
            comb[f] = mixed

    @pl.when(is_hub)
    def _():
        settle(csol, (n_hub - 1) * pair, cs_r.at[0])
        psol[...] = jnp.dot(pick[...], csol[...], preferred_element_type=F32).astype(BF16)
        for half in (0, 1):
            for f in (0, 1):

                @pl.when(sends(f))
                def _():
                    psol_copy(f, half).start()

        pair_copy().start()

    def add_face(f):
        rows = slice(f * face, (f + 1) * face)
        summed = acc[rows, :] + jnp.dot(
            onehot[f], face_in[f], preferred_element_type=F32
        )
        if f == 1:
            acc_s[...] = summed
        else:
            acc[rows, :] = summed

    base = side * nprim

    def psol_rows(m):
        return psol[pl.ds(pl.multiple_of(base + m * nprim, nprim), nprim), :]

    def finish(f, other):
        both = jnp.concatenate([psol_rows(1), other], axis=0)
        if f == 1:
            psol_s[...] = both
        else:
            rows = slice(f * face, (f + 1) * face)
            out[rows, :] = (
                acc[rows, :]
                + jnp.dot(comb[f], both, preferred_element_type=F32)
            ).astype(BF16)

    settle_near(face_in, 2, fw_r)
    add_face(2)
    add_face(3)

    @pl.when(is_leaf)
    def _():
        pair_copy().wait_recv()

    finish(2, psol_rows(0))
    finish(3, psol_rows(2))
    settle_near(face_in, 0, fw_r)
    for f in (0, 1):
        add_face(f)
        by_hub = jnp.logical_and(has[f], jnp.logical_not(corner)) if f == 1 else has[f]

        @pl.when(by_hub)
        def _():
            psol_copy(OPPOSITE[f], 0).wait_recv()

        if f == 1 and n_sx > 1:

            @pl.when(corner)
            def _():
                settle(corner_in, n_hub * nprim, corner_r.at[0])

                def add(hub, total):
                    rows = pl.ds(pl.multiple_of(hub * nprim, nprim), nprim)
                    return total + corner_in[rows, :].astype(F32)

                total = lax.fori_loop(
                    0, n_hub, add, jnp.zeros((nprim, nvec), F32), unroll=n_hub <= 4
                )
                psol_in[1] = total.astype(BF16)

        finish(f, psol_in[f])

    settle(pick, 3 * nprim, row_s.at[0])
    sent = nprim * face // nvec + face
    settle_any(res, ((both_y, 2 * sent), (one_y, sent)), near_s.at[1])
    hub_z = jnp.logical_and(both_z, is_hub)
    settle_any(
        res,
        (
            (jnp.logical_and(hub_z, jnp.logical_not(beside)), 2 * (sent + pair)),
            (jnp.logical_and(hub_z, beside), 2 * sent + pair),
            (jnp.logical_and(one_z, jnp.logical_and(is_hub, sends(0) | has[1])), sent + pair),
            (jnp.logical_and(one_z, jnp.logical_and(is_hub, jnp.logical_not(sends(0) | has[1]))), sent),
            (jnp.logical_and(both_z, is_leaf), 2 * sent),
            (jnp.logical_and(one_z, is_leaf), sent),
        ),
        near_s.at[0],
    )

    @pl.when(giver)
    def _():
        settle(corner_out, pair, corner_s.at[0])


def body(
    n_sx, n_sy,
    residual, weights, blocks, pattern, primal_basis, coarse_inverse, coarse_rows, shared_lists,
):
    ni, nvec = residual.shape[2:]
    nb, knz, blk = blocks.shape[2:5]
    nprim = primal_basis.shape[-1]
    ncr = coarse_rows.shape[-1]
    face = shared_lists.shape[-1]
    hbm = pl.BlockSpec(memory_space=pltpu.HBM)
    vmem = pl.BlockSpec(memory_space=pltpu.VMEM)
    dma = pltpu.SemaphoreType.DMA
    pair = 2 * nprim
    held_bytes = ni * nvec * 2 + face * nvec * 4 + face * pair * 2 + pair * nvec * 2
    limit = 64 * 1024 * 1024 - 65536 - held_bytes
    held = pl.pallas_call(
        functools.partial(kernel, n_sx, n_sy),
        out_shape=(
            pltpu.VMEM((ni, nvec), BF16),
            pltpu.VMEM((face, nvec), F32),
            pltpu.VMEM((face, pair), BF16),
            pltpu.VMEM((pair, nvec), BF16),
        ),
        in_specs=[hbm] * 8,
        out_specs=(vmem,) * 4,
        scratch_shapes=[
            pltpu.VMEM((ni, nvec), BF16),
            pltpu.VMEM((1, ni), F32),
            pltpu.VMEM((nprim, ni), BF16),
            pltpu.VMEM((nb, knz, blk, blk), BF16),
            pltpu.VMEM((2 * nprim, ncr), F32),
            pltpu.VMEM((1, ncr), jnp.int32),
            pltpu.VMEM((4, face), jnp.int32),
            pltpu.SMEM((knz, nb), jnp.int32),
            pltpu.VMEM((nb, blk, LANES), F32),
            pltpu.VMEM((nb, blk, nvec), BF16),
            pltpu.VMEM((ni, nvec), F32),
            pltpu.VMEM((4, face, 2 * nprim), BF16),
            pltpu.VMEM((4, face, face), BF16),
            pltpu.VMEM((2 * nprim, ncr), BF16),
            pltpu.VMEM((4 * nprim, ncr), BF16),
            pltpu.VMEM((ncr, nvec), BF16),
            pltpu.VMEM((ncr, nvec), BF16),
            pltpu.VMEM((4 * nprim, nvec), BF16),
            pltpu.VMEM((4, face, nvec), BF16),
            pltpu.VMEM((4, nprim, face), BF16),
            pltpu.VMEM((4, face, nvec), BF16),
            pltpu.VMEM((4, nprim, face), BF16),
            pltpu.VMEM((2, nprim, nvec), BF16),
            pltpu.VMEM((2 * nprim, 2 * nprim), BF16),
            pltpu.VMEM((2 * nprim, nvec), BF16),
            pltpu.VMEM((n_sy // 2 * nprim, nvec), BF16),
            dma((7,)), dma((1,)), dma((1,)), dma((2,)),
            dma((1,)), dma((1,)), dma((1,)), dma((2,)), dma((2,)), dma((2,)), dma((1,)), dma((1,)),
        ],
        compiler_params=pltpu.CompilerParams(
            collective_id=0, has_side_effects=True, vmem_limit_bytes=limit
        ),
    )(
        residual[0, 0], weights[0], blocks[0, 0], pattern[0, 0].T, primal_basis[0, 0].T,
        coarse_inverse[0], coarse_rows, shared_lists[0, 0],
    )

    def hand_over(held, acc_s, comb_s, psol_s, target, south, sem):
        rest = pl.ds(2 * face, 2 * face)
        parts = [(held, pl.ds(0, face)), (held, rest)]
        for source, at in parts:
            pltpu.make_async_copy(source.at[at], target.at[at], sem.at[0]).start()
        south[...] = (
            acc_s[...] + jnp.dot(comb_s[...], psol_s[...], preferred_element_type=F32)
        ).astype(BF16)
        pltpu.make_async_copy(south, target.at[pl.ds(face, face)], sem.at[0]).start()
        pltpu.make_async_copy(held, target, sem.at[0]).wait()

    total = pl.pallas_call(
        hand_over,
        out_shape=jax.ShapeDtypeStruct((ni, nvec), BF16),
        in_specs=[vmem] * 4,
        out_specs=hbm,
        scratch_shapes=[pltpu.VMEM((face, nvec), BF16), dma((1,))],
        compiler_params=pltpu.CompilerParams(vmem_limit_bytes=4 * 1024 * 1024),
    )(*held)
    return total[None, None]


def solution(mesh):
    return jax.shard_map(
        functools.partial(body, mesh.shape["sx"], mesh.shape["sy"]),
        mesh=mesh,
        in_specs=(
            P("sx", "sy", None, None),
            P("sx", "sy", None),
            P("sx", "sy", None, None, None, None),
            P("sx", "sy", None, None),
            P("sx", "sy", None, None),
            P("sx", "sy", None),
            P("sx", None),
            P("sx", "sy", None, None),
        ),
        out_specs=P("sx", "sy", None, None),
        check_vma=False,
    )
```
